1024 devices in a mesh: lat: 32 (over y_hi, z), lon: 32 (over y_lo, x, core).
Axes of the slice: x: 4, y: 8 (y_hi: 2, y_lo: 4; y = y_hi * 4 + y_lo), z: 16, core: 2. Of those that a mesh axis runs over, the one named last changes fastest.
Arguments:
- query_field: bfloat16 [256, 512, 768], P('lat', 'lon'), may hold values from -6 to 6
- key_field: bfloat16 [256, 512, 768], P('lat', 'lon'), may hold values from -6 to 6
- value_field: bfloat16 [256, 512, 768], P('lat', 'lon'), may hold values from -12 to 12
- out_cotangent: bfloat16 [256, 512, 768], P('lat', 'lon'), may hold values from -16 to 16
Outputs:
- attended: bfloat16 [256, 512, 768], P('lat', 'lon')
- query_grad: bfloat16 [256, 512, 768], P('lat', 'lon')
- key_grad: bfloat16 [256, 512, 768], P('lat', 'lon')
- value_grad: bfloat16 [256, 512, 768], P('lat', 'lon')
The draws below stay inside these ranges and needn't reach their ends.
All inputs are finite; a program needn't handle non-finite values.
Results may differ from the reference program's by a relative error of at most 0.025.
Values may be sent and summed in bfloat16 or wider, within the bound.
No kernel may reach another device: no remote copies, remote signals or barrier semaphores. Data moves between devices by JAX's collectives and lax.ppermute only.
A program may use at most 128 MiB of HBM per device.

```python
import jax
import jax.numpy as jnp
from jax import lax

D = 768
HEADS = 12
HEAD_DIM = 64
TILE = 8
LAT = 256
LON = 512


def draw_query_field(key, part):
    drawn = jnp.clip(1.5 * jax.random.normal(jax.random.fold_in(key, 11), (LAT, LON, D), jnp.float32), -6.0, 6.0)
    return drawn.astype(jnp.bfloat16)


def draw_key_field(key, part):
    drawn = jnp.clip(jax.random.normal(jax.random.fold_in(key, 13), (LAT, LON, D), jnp.float32), -4.0, 4.0)
    return drawn.astype(jnp.bfloat16)


def steps_of(stream_key, shape, cuts, low, top_value):
    loudness, own = 1.0, jax.random.fold_in(stream_key, 6)
    for axis_at, shards_of in cuts:
        draws = jnp.exp(jax.random.uniform(jax.random.fold_in(own, axis_at), (shards_of,), jnp.float32, low / len(cuts), top_value / len(cuts)))
        loudness = loudness * jnp.repeat(draws, shape[axis_at] // shards_of).reshape([-1 if axis == axis_at else 1 for axis in range(len(shape))])
    return loudness


def gaussian(rng, extent, deviation, limit, pieces=(), kind=jnp.bfloat16):
    level = steps_of(rng, extent, pieces, -0.22, 0.18) if pieces else 1.0
    drawn = jax.random.normal(rng, extent, jnp.float32) * deviation * level
    return jnp.minimum(jnp.maximum(drawn, -limit), limit).astype(kind)


def setup_inputs(seed: int = 0) -> dict:
    keys = jax.random.split(jax.random.key(seed), 5)
    query_field = draw_query_field(jax.random.fold_in(keys[4], 71), 0)
    key_field = draw_key_field(jax.random.fold_in(keys[4], 71), 0)
    value_field = gaussian(keys[2], (LAT, LON, D), 3.0, 12.0, ((0, 32), (1, 32)))
    out_cotangent = gaussian(keys[3], (LAT, LON, D), 4.0, 16.0, ((0, 32), (1, 32)))
    return {"query_field": query_field, "key_field": key_field, "value_field": value_field, "out_cotangent": out_cotangent}


def tiles_of(grid, head_count):
    grid_rows, grid_cols, features = grid.shape
    shaped = grid.reshape(grid_rows // TILE, TILE, grid_cols // TILE, TILE, head_count, features // head_count)
    return shaped.transpose(0, 2, 1, 3, 4, 5).reshape(grid_rows // TILE, grid_cols // TILE, TILE * TILE, head_count, features // head_count)


def grid_of(tiles):
    tile_rows, tile_cols, cells, head_count, features = tiles.shape
    shaped = tiles.reshape(tile_rows, tile_cols, TILE, TILE, head_count * features)
    return shaped.transpose(0, 2, 1, 3, 4).reshape(tile_rows * TILE, tile_cols * TILE, head_count * features)


def pad_tiles(tiles):
    looped = jnp.concatenate([tiles[:, -1:], tiles, tiles[:, :1]], axis=1)
    widths = [(1, 1)] + [(0, 0)] * (tiles.ndim - 1)
    return jnp.pad(looped, widths)


def settle(values):
    return lax.optimization_barrier(values.astype(jnp.bfloat16)).astype(jnp.float32)


def reference(query_field, key_field, value_field, out_cotangent):
    scaling = HEAD_DIM ** -0.5
    query_tiles = tiles_of(query_field, HEADS)
    key_tiles = tiles_of(key_field, HEADS)
    value_tiles = tiles_of(value_field, HEADS)
    grad_tiles = tiles_of(out_cotangent, HEADS)
    lat_tiles, lon_tiles = query_tiles.shape[0], query_tiles.shape[1]
    padded_keys = pad_tiles(key_tiles)
    padded_values = pad_tiles(value_tiles)
    offsets = [(step_lat, step_lon) for step_lat in range(3) for step_lon in range(3)]

    def query_row(tile_row):
        queries = lax.dynamic_index_in_dim(query_tiles, tile_row, 0, keepdims=False).astype(jnp.float32)
        cotangent = lax.dynamic_index_in_dim(grad_tiles, tile_row, 0, keepdims=False).astype(jnp.float32)
        key_rows, value_rows, scores = [], [], []
        for step_lat, step_lon in offsets:
            keys_here = lax.dynamic_index_in_dim(padded_keys, tile_row + step_lat, 0, keepdims=False)[step_lon:step_lon + lon_tiles].astype(jnp.float32)
            values_here = lax.dynamic_index_in_dim(padded_values, tile_row + step_lat, 0, keepdims=False)[step_lon:step_lon + lon_tiles].astype(jnp.float32)
            key_rows.append(keys_here)
            value_rows.append(values_here)
            score_part = jnp.einsum('bqhd,bkhd->bhqk', queries, keys_here) * scaling
            valid = (tile_row + step_lat - 1 >= 0) & (tile_row + step_lat - 1 < lat_tiles)
            scores.append(jnp.where(valid, score_part, -jnp.inf))
        scores = jnp.stack(scores)
        peak = jnp.max(scores, axis=(0, 4), keepdims=True)
        log_total = peak + jnp.log(jnp.sum(jnp.exp(scores - peak), axis=(0, 4), keepdims=True))
        weights = jnp.exp(scores - log_total)
        blended = jnp.zeros(queries.shape, jnp.float32)
        for offset_index in range(9):
            blended = blended + jnp.einsum('bhqk,bkhd->bqhd', settle(weights[offset_index]), value_rows[offset_index])
        attended_row = blended.astype(jnp.bfloat16)
        row_drift = jnp.sum(cotangent * lax.optimization_barrier(attended_row).astype(jnp.float32), axis=-1)
        drift_cols = jnp.swapaxes(row_drift, 1, 2)[..., None]
        query_sum = jnp.zeros(queries.shape, jnp.float32)
        for offset_index in range(9):
            products = jnp.einsum('bqhd,bkhd->bhqk', cotangent, value_rows[offset_index])
            slopes = settle(weights[offset_index] * (products - drift_cols))
            query_sum = query_sum + jnp.einsum('bhqk,bkhd->bqhd', slopes, key_rows[offset_index])
        lse_row = jnp.swapaxes(log_total[0, :, :, :, 0], 1, 2)
        return attended_row, (query_sum * scaling).astype(jnp.bfloat16), lse_row, row_drift

    rows_index = jnp.arange(lat_tiles, dtype=jnp.int32)
    attended_tiles, query_grad_tiles, lse_tiles, drift_tiles = lax.map(query_row, rows_index)
    padded_queries = pad_tiles(query_tiles)
    padded_grads = pad_tiles(grad_tiles)
    padded_lse = pad_tiles(lse_tiles[..., None])
    padded_drift = pad_tiles(drift_tiles[..., None])

    def key_row(tile_row):
        keys_own = lax.dynamic_index_in_dim(key_tiles, tile_row, 0, keepdims=False).astype(jnp.float32)
        values_own = lax.dynamic_index_in_dim(value_tiles, tile_row, 0, keepdims=False).astype(jnp.float32)
        key_sum = jnp.zeros(keys_own.shape, jnp.float32)
        value_sum = jnp.zeros(keys_own.shape, jnp.float32)
        for step_lat, step_lon in offsets:
            def pick(padded):
                return lax.dynamic_index_in_dim(padded, tile_row + step_lat, 0, keepdims=False)[step_lon:step_lon + lon_tiles]
            queries = pick(padded_queries).astype(jnp.float32)
            cotangent = pick(padded_grads).astype(jnp.float32)
            lse_cols = jnp.swapaxes(pick(padded_lse)[..., 0], 1, 2)[..., None]
            drift_cols = jnp.swapaxes(pick(padded_drift)[..., 0], 1, 2)[..., None]
            valid = (tile_row + step_lat - 1 >= 0) & (tile_row + step_lat - 1 < lat_tiles)
            score_part = jnp.einsum('bqhd,bkhd->bhqk', queries, keys_own) * scaling
            chance = jnp.where(valid, jnp.exp(score_part - lse_cols), jnp.zeros(score_part.shape, jnp.float32))
            products = jnp.einsum('bqhd,bkhd->bhqk', cotangent, values_own)
            slopes = settle(chance * (products - drift_cols))
            key_sum = key_sum + jnp.einsum('bhqk,bqhd->bkhd', slopes, queries)
            value_sum = value_sum + jnp.einsum('bhqk,bqhd->bkhd', settle(chance), cotangent)
        return (key_sum * scaling).astype(jnp.bfloat16), value_sum.astype(jnp.bfloat16)

    key_grad_tiles, value_grad_tiles = lax.map(key_row, rows_index)
    return grid_of(attended_tiles), grid_of(query_grad_tiles), grid_of(key_grad_tiles), grid_of(value_grad_tiles)
```

```python
import jax
import jax.numpy as jnp
from jax import lax
from jax.experimental import pallas as pl
from jax.experimental.pallas import tpu as pltpu
from jax.sharding import PartitionSpec as P

HEAD_DIM = 64
TILE = 8
PAIR = 2 * HEAD_DIM
FAR = -1e30


def dot(a, b):
    return jnp.dot(a, b, preferred_element_type=jnp.float32)


def tile_order(x):
    width = x.shape[-1]
    return jnp.concatenate(
        [x[:, :TILE].reshape(TILE * TILE, width), x[:, TILE:].reshape(TILE * TILE, width)], axis=0
    )


def grid_order(x):
    width = x.shape[-1]
    half = TILE * TILE
    return jnp.concatenate(
        [x[:half].reshape(TILE, TILE, width), x[half:].reshape(TILE, TILE, width)], axis=1
    )


def attend_kernel(
    bias_ref, q_ref, g_ref, own_ref, north_ref, south_ref, west_ref, east_ref,
    att_ref, dq_ref, mid_ref, up_ref, down_ref, left_ref, right_ref,
):
    f32, bf16 = jnp.float32, jnp.bfloat16
    north_bias, south_bias = bias_ref[0], bias_ref[1]

    def keys(which):
        rows = [ref[which].reshape(PAIR, PAIR) for ref in (north_ref, own_ref, south_ref)]
        sides = [
            ref[which].astype(f32).reshape(3 * TILE * TILE, PAIR).astype(bf16)
            for ref in (west_ref, east_ref)
        ]
        return jnp.concatenate(rows + sides, axis=0)

    k_all, v_all = keys(0), keys(1)
    q_nat = tile_order(q_ref[...].astype(f32)) * (HEAD_DIM**-0.5)
    g_nat = tile_order(g_ref[...].astype(f32))
    q_turn, g_turn = q_nat.T, g_nat.T
    row = lax.broadcasted_iota(jnp.int32, (PAIR, PAIR), 0) < HEAD_DIM
    lane = lax.broadcasted_iota(jnp.int32, (PAIR, PAIR), 1) < HEAD_DIM

    def wide(x):
        return jnp.concatenate([jnp.where(row, x, 0.0), jnp.where(row, 0.0, x)], axis=1).astype(bf16)

    def tall(x):
        return jnp.concatenate([jnp.where(lane, x, 0.0), jnp.where(lane, 0.0, x)], axis=0).astype(bf16)

    core, side = 3 * PAIR, 3 * TILE * TILE
    in_west = (lax.broadcasted_iota(jnp.int32, (side, 2 * PAIR), 1) & HEAD_DIM) == 0

    def near(x):
        return jnp.concatenate(
            [x[:core], jnp.where(in_west, x[core : core + side], x[core + side :])], axis=0
        )

    def full(x):
        rest = x[core:]
        return jnp.concatenate(
            [x[:core], jnp.where(in_west, rest, 0.0), jnp.where(in_west, 0.0, rest)], axis=0
        ).astype(bf16)

    def diagonal(x):
        return jnp.concatenate([x[:HEAD_DIM, :PAIR], x[HEAD_DIM:, PAIR:]], axis=0)

    scores = near(dot(k_all, wide(q_turn)))
    half = TILE * TILE
    scores = jnp.concatenate(
        [
            scores[:PAIR] + north_bias,
            scores[PAIR : 2 * PAIR],
            scores[2 * PAIR : core] + south_bias,
            scores[core : core + half] + north_bias,
            scores[core + half : core + 2 * half],
            scores[core + 2 * half :] + south_bias,
        ],
        axis=0,
    )
    peak = jnp.max(scores, axis=0, keepdims=True)
    raised = jnp.exp(scores - peak)
    weights = raised * (1.0 / jnp.sum(raised, axis=0, keepdims=True))
    low = full(weights)
    att_turn = diagonal(dot(v_all.T, low)).astype(bf16).astype(f32)
    att_ref[...] = grid_order(att_turn.T).astype(bf16)
    product = g_turn * att_turn
    drift = jnp.concatenate(
        [
            jnp.sum(product[:HEAD_DIM], axis=0, keepdims=True),
            jnp.sum(product[HEAD_DIM:], axis=0, keepdims=True),
        ],
        axis=1,
    )
    slopes = full(weights * (near(dot(v_all, wide(g_turn))) - drift))
    dq_turn = diagonal(dot(k_all.T, slopes)) * (HEAD_DIM**-0.5)
    dq_ref[...] = grid_order(dq_turn.T).astype(bf16)
    for which, terms in ((0, dot(slopes, tall(q_nat))), (1, dot(low, tall(g_nat)))):
        up_ref[which] = terms[:PAIR].reshape(TILE, 2 * TILE, PAIR).astype(bf16)
        mid_ref[which] = terms[PAIR : 2 * PAIR].reshape(TILE, 2 * TILE, PAIR)
        down_ref[which] = terms[2 * PAIR : core].reshape(TILE, 2 * TILE, PAIR).astype(bf16)
        left_ref[which] = terms[core : core + side].reshape(3 * TILE, TILE, PAIR).astype(bf16)
        right_ref[which] = terms[core + side :].reshape(3 * TILE, TILE, PAIR).astype(bf16)


def attend(bias, q, g, own, north, south, west, east):
    width = q.shape[-1]
    grid3 = pl.BlockSpec((TILE, 2 * TILE, PAIR), lambda p: (0, 0, p))
    grid4 = pl.BlockSpec((2, TILE, 2 * TILE, PAIR), lambda p: (0, 0, 0, p))
    side4 = pl.BlockSpec((2, 3 * TILE, TILE, PAIR), lambda p: (0, 0, 0, p))
    shape = jax.ShapeDtypeStruct
    rows, cols = (2, TILE, 2 * TILE, width), (2, 3 * TILE, TILE, width)
    return pl.pallas_call(
        attend_kernel,
        grid=(width // PAIR,),
        in_specs=[pl.BlockSpec(memory_space=pltpu.SMEM), grid3, grid3, grid4, grid4, grid4, side4, side4],
        out_specs=[grid3, grid3, grid4, grid4, grid4, side4, side4],
        out_shape=[
            shape(q.shape, jnp.bfloat16),
            shape(q.shape, jnp.bfloat16),
            shape(rows, jnp.float32),
            shape(rows, jnp.bfloat16),
            shape(rows, jnp.bfloat16),
            shape(cols, jnp.bfloat16),
            shape(cols, jnp.bfloat16),
        ],
        compiler_params=pltpu.CompilerParams(vmem_limit_bytes=48 << 20),
        cost_estimate=pl.CostEstimate(flops=1 << 31, bytes_accessed=12 << 20, transcendentals=1 << 20),
        name="attend",
    )(bias, q, g, own, north, south, west, east)


def ring(value, steps):
    count = lax.axis_size("lon")
    return lax.ppermute(value, "lon", [(i, (i + steps) % count) for i in range(count)])


def line(value, steps):
    count = lax.axis_size("lat")
    first, last = max(0, -steps), min(count, count - steps)
    return lax.ppermute(value, "lat", [(i, i + steps) for i in range(first, last)])


def shards(query_field, key_field, value_field, out_cotangent):
    band = lax.axis_index("lat")
    bias = jnp.stack(
        [
            jnp.where(band == 0, FAR, 0.0),
            jnp.where(band == lax.axis_size("lat") - 1, FAR, 0.0),
        ]
    ).astype(jnp.float32)
    own = jnp.stack([key_field, value_field])
    north, south = line(own, 1), line(own, -1)
    first = jnp.concatenate([x[:, :, :TILE] for x in (north, own, south)], axis=1)
    second = jnp.concatenate([x[:, :, TILE:] for x in (north, own, south)], axis=1)
    west, east = ring(second, 1), ring(first, -1)
    att, dq, mid, up, down, left, right = attend(
        bias, query_field, out_cotangent, own, north, south, west, east
    )
    to_second, to_first = ring(left, -1), ring(right, 1)
    spread = jnp.concatenate([to_first, to_second], axis=2).astype(jnp.float32)
    up = (up.astype(jnp.float32) + spread[:, :TILE]).astype(jnp.bfloat16)
    down = (down.astype(jnp.float32) + spread[:, 2 * TILE :]).astype(jnp.bfloat16)
    from_south, from_north = line(up, -1), line(down, 1)
    total = (
        mid
        + spread[:, TILE : 2 * TILE]
        + from_south.astype(jnp.float32)
        + from_north.astype(jnp.float32)
    ).astype(jnp.bfloat16)
    return att, dq, total[0], total[1]


def solution(mesh):
    spec = P("lat", "lon", None)
    return jax.shard_map(
        shards, mesh=mesh, in_specs=(spec,) * 4, out_specs=(spec,) * 4, check_vma=False
    )
```

```python
import jax
import jax.numpy as jnp
from jax import lax
from jax.experimental import pallas as pl
from jax.experimental.pallas import tpu as pltpu
from jax.sharding import PartitionSpec as P

HEAD_DIM = 64
TILE = 8
CELLS = TILE * TILE
PAIR = 2 * HEAD_DIM
CORE = 6 * CELLS
SIDE = 3 * CELLS
SCALE = HEAD_DIM**-0.5
FAR = -1e30


def dot(a, b):
    return jnp.dot(a, b, preferred_element_type=jnp.float32)


def tile_order(x, odd):
    west = x[:, :TILE].reshape(CELLS, x.shape[-1])
    east = x[:, TILE:].reshape(CELLS, x.shape[-1])
    return jnp.concatenate([jnp.where(odd, west, east), jnp.where(odd, east, west)], axis=0)


def grid_order(x, odd):
    first = x[:CELLS].reshape(TILE, TILE, x.shape[-1])
    second = x[CELLS:].reshape(TILE, TILE, x.shape[-1])
    return jnp.concatenate([jnp.where(odd, first, second), jnp.where(odd, second, first)], axis=1)


def wide(x):
    row = lax.broadcasted_iota(jnp.int32, (PAIR, PAIR), 0) < HEAD_DIM
    return jnp.concatenate([jnp.where(row, x, 0.0), jnp.where(row, 0.0, x)], axis=1).astype(jnp.bfloat16)


def beside_first(rows):
    return (lax.broadcasted_iota(jnp.int32, (rows, 2 * PAIR), 1) & CELLS) == 0


def near(x):
    sides = jnp.where(beside_first(SIDE), x[CORE : CORE + SIDE], x[CORE + SIDE :])
    return jnp.concatenate([x[:CORE], sides], axis=0)


def full(x):
    sides, first = x[CORE:], beside_first(SIDE)
    return jnp.concatenate(
        [x[:CORE], jnp.where(first, sides, 0.0), jnp.where(first, 0.0, sides)], axis=0
    ).astype(jnp.bfloat16)


def diagonal(x):
    return jnp.concatenate([x[:HEAD_DIM, :PAIR], x[HEAD_DIM:, PAIR:]], axis=0)


def masked(x, bias):
    a, b, c = 4 * CELLS, CORE, CORE + 2 * CELLS
    return jnp.concatenate([x[:a], x[a:b] + bias, x[b:c], x[c:] + bias], axis=0)


def by_head(x):
    return jnp.concatenate(
        [
            jnp.sum(x[:HEAD_DIM], axis=0, keepdims=True),
            jnp.sum(x[HEAD_DIM:], axis=0, keepdims=True),
        ],
        axis=1,
    )


def gather(which, odd, bands, sides):
    rows = [tile_order(ref[which].astype(jnp.float32), odd) for ref in bands]
    rows += [ref[which].astype(jnp.float32).reshape(SIDE, PAIR) for ref in sides]
    return jnp.concatenate(rows, axis=0)


def query_kernel(
    bias_ref, odd_ref, mine_ref, own_ref, even_ref, odds_ref, first_ref, second_ref, att_ref, dq_ref, stats_ref
):
    f32, bf16 = jnp.float32, jnp.bfloat16
    odd = odd_ref[0] == 1
    bands, sides = (own_ref, even_ref, odds_ref), (first_ref, second_ref)
    k_all = gather(0, odd, bands, sides).astype(bf16)
    v_all = gather(1, odd, bands, sides).astype(bf16)
    q_turn = (tile_order(mine_ref[0].astype(f32), odd) * SCALE).T
    g_turn = tile_order(mine_ref[1].astype(f32), odd).T
    scores = masked(near(dot(k_all, wide(q_turn))), bias_ref[0])
    peak = jnp.max(scores, axis=0, keepdims=True)
    raised = jnp.exp(scores - peak)
    total = jnp.sum(raised, axis=0, keepdims=True)
    weights = raised * (1.0 / total)
    att_turn = diagonal(dot(v_all.T, full(weights))).astype(bf16).astype(f32)
    att_ref[...] = grid_order(att_turn.T, odd).astype(bf16)
    drift = by_head(g_turn * att_turn)
    slopes = full(weights * (near(dot(v_all, wide(g_turn))) - drift))
    dq_turn = diagonal(dot(k_all.T, slopes)) * SCALE
    dq_ref[...] = grid_order(dq_turn.T, odd).astype(bf16)
    log_total = peak + jnp.log(total)
    stats_ref[0] = jnp.concatenate(
        [log_total[:, :PAIR], log_total[:, PAIR:], drift[:, :PAIR], drift[:, PAIR:], jnp.zeros((4, PAIR), f32)],
        axis=0,
    )


def key_kernel(
    bias_ref, odd_ref, mine_ref, own_ref, even_ref, odds_ref, first_ref, second_ref,
    own_stats, even_stats, odds_stats, first_stats, second_stats, dk_ref, dv_ref,
):
    f32, bf16 = jnp.float32, jnp.bfloat16
    odd = odd_ref[0] == 1
    bands, sides = (own_ref, even_ref, odds_ref), (first_ref, second_ref)
    q_all = (gather(0, odd, bands, sides) * SCALE).astype(bf16)
    g_all = gather(1, odd, bands, sides).astype(bf16)
    k_turn = tile_order(mine_ref[0].astype(f32), odd).T
    v_turn = tile_order(mine_ref[1].astype(f32), odd).T
    stats = [own_stats[0], even_stats[0], odds_stats[0]]
    stats += [ref[band, 0] for ref in (first_stats, second_stats) for band in range(3)]
    turned = jnp.concatenate(stats + [jnp.zeros((PAIR - 8 * 9, PAIR), f32)], axis=0).T

    def columns(base):
        def piece(at, low, high):
            col = 8 * at + base
            return jnp.concatenate(
                [
                    jnp.broadcast_to(turned[low:high, col : col + 1], (high - low, PAIR)),
                    jnp.broadcast_to(turned[low:high, col + 1 : col + 2], (high - low, PAIR)),
                ],
                axis=1,
            )

        core = [piece(at, 0, PAIR) for at in range(3)]
        choose = beside_first(CELLS)
        rest = [
            jnp.where(choose, piece(3 + band, 0, CELLS), piece(6 + band, CELLS, PAIR)) for band in range(3)
        ]
        return jnp.concatenate(core + rest, axis=0)

    scores = masked(near(dot(q_all, wide(k_turn))), bias_ref[0])
    weights = jnp.exp(scores - columns(0))
    dv_turn = diagonal(dot(g_all.T, full(weights)))
    dv_ref[...] = grid_order(dv_turn.T, odd).astype(bf16)
    slopes = full(weights * (near(dot(g_all, wide(v_turn))) - columns(2)))
    dk_turn = diagonal(dot(q_all.T, slopes))
    dk_ref[...] = grid_order(dk_turn.T, odd).astype(bf16)


SCALAR = pl.BlockSpec(memory_space=pltpu.SMEM)
GRID3 = pl.BlockSpec((TILE, 2 * TILE, PAIR), lambda p: (0, 0, p))
GRID4 = pl.BlockSpec((2, TILE, 2 * TILE, PAIR), lambda p: (0, 0, 0, p))
SIDE4 = pl.BlockSpec((2, 3 * TILE, TILE, PAIR), lambda p: (0, 0, 0, p))
STATS = pl.BlockSpec((1, 8, PAIR), lambda p: (p, 0, 0))
STATS3 = pl.BlockSpec((3, 1, 8, PAIR), lambda p: (0, p, 0, 0))
COST = pl.CostEstimate(flops=1 << 31, bytes_accessed=12 << 20, transcendentals=1 << 20)


def call(kernel, name, extra_specs, out_specs, out_shape, args):
    width = args[2].shape[-1]
    return pl.pallas_call(
        kernel,
        grid=(width // PAIR,),
        in_specs=[SCALAR, SCALAR, GRID4, GRID4, GRID4, GRID4, SIDE4, SIDE4, *extra_specs],
        out_specs=out_specs,
        out_shape=out_shape,
        compiler_params=pltpu.CompilerParams(vmem_limit_bytes=48 << 20),
        cost_estimate=COST,
        name=name,
    )(*args)


def pack_kernel(odd_ref, own_ref, even_ref, odds_ref, first_ref, second_ref):
    odd = odd_ref[0] == 1
    for band, ref in enumerate((own_ref, even_ref, odds_ref)):
        x = ref[0].astype(jnp.float32)
        west, east = x[:, :TILE], x[:, TILE:]
        rows = pl.ds(band * TILE, TILE)
        first_ref[0, rows] = jnp.where(odd, west, east).astype(jnp.bfloat16)
        second_ref[0, rows] = jnp.where(odd, east, west).astype(jnp.bfloat16)


def pack(odd, own, even, odds):
    width = own.shape[-1]
    band = pl.BlockSpec((1, TILE, 2 * TILE, width), lambda i: (i, 0, 0, 0))
    side = pl.BlockSpec((1, 3 * TILE, TILE, width), lambda i: (i, 0, 0, 0))
    shape = jax.ShapeDtypeStruct((2, 3 * TILE, TILE, width), jnp.bfloat16)
    return pl.pallas_call(
        pack_kernel,
        grid=(2,),
        in_specs=[SCALAR, band, band, band],
        out_specs=[side, side],
        out_shape=[shape, shape],
        cost_estimate=pl.CostEstimate(flops=1 << 20, bytes_accessed=5 << 20, transcendentals=0),
        name="pack",
    )(odd, own, even, odds)


def swap(value, axis, start, closed):
    count = lax.axis_size(axis)
    pairs = []
    for low in range(start, count if closed else count - 1, 2):
        high = (low + 1) % count
        pairs += [(low, high), (high, low)]
    return lax.ppermute(value, axis, pairs)


def shards(query_field, key_field, value_field, out_cotangent):
    band = lax.axis_index("lat")
    edge = (band == 0) | (band == lax.axis_size("lat") - 1)
    bias = jnp.where(edge, FAR, 0.0).astype(jnp.float32)[None]
    odd = (lax.axis_index("lon") % 2).astype(jnp.int32)[None]
    keys = jnp.stack([key_field, value_field])
    keys_even, keys_odd = swap(keys, "lat", 0, False), swap(keys, "lat", 1, False)
    queries = jnp.stack([query_field, out_cotangent])
    queries_even, queries_odd = swap(queries, "lat", 0, False), swap(queries, "lat", 1, False)
    first, second = pack(odd, keys, keys_even, keys_odd)
    keys_first, keys_second = swap(first, "lon", 0, True), swap(second, "lon", 1, True)
    first, second = pack(odd, queries, queries_even, queries_odd)
    queries_first, queries_second = swap(first, "lon", 0, True), swap(second, "lon", 1, True)
    shape = jax.ShapeDtypeStruct
    field = shape(query_field.shape, jnp.bfloat16)
    pairs = query_field.shape[-1] // PAIR
    att, dq, stats = call(
        query_kernel, "queries", [], [GRID3, GRID3, STATS],
        [field, field, shape((pairs, 8, PAIR), jnp.float32)],
        (bias, odd, queries, keys, keys_even, keys_odd, keys_first, keys_second),
    )
    stats_even, stats_odd = swap(stats, "lat", 0, False), swap(stats, "lat", 1, False)
    column = jnp.stack([stats, stats_even, stats_odd])
    stats_first, stats_second = swap(column, "lon", 0, True), swap(column, "lon", 1, True)
    dk, dv = call(
        key_kernel, "keys", [STATS, STATS, STATS, STATS3, STATS3], [GRID3, GRID3], [field, field],
        (
            bias, odd, keys, queries, queries_even, queries_odd, queries_first, queries_second,
            stats, stats_even, stats_odd, stats_first, stats_second,
        ),
    )
    return att, dq, dk, dv


def solution(mesh):
    spec = P("lat", "lon", None)
    return jax.shard_map(
        shards, mesh=mesh, in_specs=(spec,) * 4, out_specs=(spec,) * 4, check_vma=False
    )
```

```python
import jax
import jax.numpy as jnp
from jax import lax
from jax.experimental import pallas as pl
from jax.experimental.pallas import tpu as pltpu
from jax.sharding import PartitionSpec as P

HEAD_DIM = 64
TILE = 8
CELLS = TILE * TILE
BAND = 2 * CELLS
PAIR = 2 * HEAD_DIM
SCALE = HEAD_DIM**-0.5
FAR = -1e30
F32, BF16 = jnp.float32, jnp.bfloat16


def dot(a, b):
    return jnp.dot(a, b, preferred_element_type=F32)


def tile_order(x, odd):
    west = x[:, :TILE].reshape(CELLS, x.shape[-1])
    east = x[:, TILE:].reshape(CELLS, x.shape[-1])
    return jnp.concatenate([jnp.where(odd, west, east), jnp.where(odd, east, west)], axis=0)


def grid_order(x, odd):
    first = x[:CELLS].reshape(TILE, TILE, x.shape[-1])
    second = x[CELLS:].reshape(TILE, TILE, x.shape[-1])
    return jnp.concatenate([jnp.where(odd, first, second), jnp.where(odd, second, first)], axis=1)


def below(shape, axis, bound):
    return lax.broadcasted_iota(jnp.int32, shape, axis) < bound


def wide(x):
    row = below(x.shape, 0, HEAD_DIM)
    return jnp.concatenate([jnp.where(row, x, 0.0), jnp.where(row, 0.0, x)], axis=1).astype(BF16)


def diagonal(x):
    return jnp.concatenate([x[:HEAD_DIM, :PAIR], x[HEAD_DIM:, PAIR : 2 * PAIR]], axis=0)


def by_head(x):
    return jnp.concatenate(
        [
            jnp.sum(x[:HEAD_DIM], axis=0, keepdims=True),
            jnp.sum(x[HEAD_DIM:], axis=0, keepdims=True),
        ],
        axis=1,
    )


def each_pair(width, step):
    def body(p, carry):
        step(p, pl.ds(pl.multiple_of(p * PAIR, PAIR), PAIR))
        return carry

    lax.fori_loop(0, width // PAIR, body, 0)


def query_kernel(
    bias_ref, odd_ref, mine_ref, own_ref, even_ref, odds_ref, first_ref, second_ref, att_ref, dq_ref, stats_ref
):
    odd = odd_ref[0] == 1
    core, side = 3 * BAND, 3 * CELLS
    refs = (own_ref, even_ref, odds_ref, first_ref, second_ref)

    def step(p, lanes):
        beside_first = (lax.broadcasted_iota(jnp.int32, (side, 2 * PAIR), 1) & CELLS) == 0

        def near(x):
            return jnp.concatenate(
                [x[:core], jnp.where(beside_first, x[core : core + side], x[core + side :])], axis=0
            )

        def full(x):
            rest = x[core:]
            return jnp.concatenate(
                [x[:core], jnp.where(beside_first, rest, 0.0), jnp.where(beside_first, 0.0, rest)], axis=0
            ).astype(BF16)

        k_all = jnp.concatenate([ref[0, :, lanes] for ref in refs], axis=0)
        v_all = jnp.concatenate([ref[1, :, lanes] for ref in refs], axis=0)
        q_turn = mine_ref[0, :, lanes].astype(F32).T
        g_turn = mine_ref[1, :, lanes].astype(F32).T
        scores = near(dot(k_all, wide(q_turn)))
        cut, last = 2 * BAND, core + 2 * CELLS
        bias = bias_ref[0]
        scores = jnp.concatenate(
            [scores[:cut], scores[cut:core] + bias, scores[core:last], scores[last:] + bias], axis=0
        )
        peak = jnp.max(scores, axis=0, keepdims=True)
        raised = jnp.exp(scores - peak)
        total = jnp.sum(raised, axis=0, keepdims=True)
        weights = raised * (1.0 / total)
        att_turn = diagonal(dot(v_all.T, full(weights))).astype(BF16).astype(F32)
        att_ref[:, :, lanes] = grid_order(att_turn.T, odd).astype(BF16)
        drift = by_head(g_turn * att_turn)
        log_total = peak + jnp.log(total)
        stats_ref[p] = jnp.concatenate(
            [log_total[:, :PAIR], log_total[:, PAIR:], drift[:, :PAIR], drift[:, PAIR:], jnp.zeros((4, PAIR), F32)],
            axis=0,
        )
        slopes = full(weights * (near(dot(v_all, wide(g_turn))) - drift))
        dq_turn = diagonal(dot(k_all.T, slopes)) * SCALE
        dq_ref[:, :, lanes] = grid_order(dq_turn.T, odd).astype(BF16)

    each_pair(mine_ref.shape[-1], step)


def key_kernel(
    bias_ref, own_ref, first_ref, second_ref, mine_ref, even_ref, odds_ref, mine_stats, even_stats, odds_stats,
    mid_ref, to_first_ref, to_second_ref,
):
    refs = (mine_ref, even_ref, odds_ref)

    def step(p, lanes):
        low_lane = below((PAIR, PAIR), 1, CELLS)
        low_row = below((PAIR, PAIR), 0, HEAD_DIM)

        def keys(which):
            own = own_ref[which, :, lanes].astype(F32).T
            both = jnp.concatenate(
                [first_ref[which, :CELLS, lanes], second_ref[which, :CELLS, lanes]], axis=0
            ).astype(F32).T
            turned = pltpu.roll(both, CELLS, axis=1)
            block = low_row == low_lane
            first = jnp.where(block, jnp.where(low_lane, both, turned), 0.0).astype(BF16)
            second = jnp.where(block, jnp.where(low_lane, turned, both), 0.0).astype(BF16)
            return jnp.concatenate([wide(own), first, second], axis=1)

        def near(x):
            sides = [
                x[at * CELLS : (at + 1) * CELLS, (2 + at % 2) * PAIR : (3 + at % 2) * PAIR] for at in range(6)
            ]
            return jnp.concatenate([x[:, : 2 * PAIR], jnp.concatenate(sides, axis=0)], axis=1)

        def full(x):
            x = x.astype(BF16)
            none = jnp.zeros((CELLS, PAIR), BF16)
            sides = [x[at * CELLS : (at + 1) * CELLS, 2 * PAIR :] for at in range(6)]
            first = jnp.concatenate([none if at % 2 else sides[at] for at in range(6)], axis=0)
            second = jnp.concatenate([sides[at] if at % 2 else none for at in range(6)], axis=0)
            return jnp.concatenate([x[:, : 2 * PAIR], first, second], axis=1)

        stats = [ref[p] for ref in (mine_stats, even_stats, odds_stats)]
        columns = jnp.concatenate(stats + [jnp.zeros((PAIR - 24, PAIR), F32)], axis=0).T

        def column(base):
            rows = []
            for at in range(3):
                head0 = jnp.broadcast_to(columns[:, 8 * at + base : 8 * at + base + 1], (PAIR, PAIR))
                head1 = jnp.broadcast_to(columns[:, 8 * at + base + 1 : 8 * at + base + 2], (PAIR, PAIR))
                rows.append(jnp.concatenate([head0, head1, jnp.where(low_lane, head0, head1)], axis=1))
            return jnp.concatenate(rows, axis=0)

        def store(which, x):
            mid_ref[which, :, lanes] = diagonal(x).T
            first, second = x[:, 2 * PAIR : 3 * PAIR], x[:, 3 * PAIR :]
            first = jnp.where(low_row, first, pltpu.roll(first, CELLS, axis=1))
            second = jnp.where(low_row, pltpu.roll(second, CELLS, axis=1), second)
            both = jnp.where(low_lane, first, second).T.astype(BF16)
            to_first_ref[which, :, lanes] = both[:CELLS]
            to_second_ref[which, :, lanes] = both[CELLS:]

        q_all = jnp.concatenate([ref[0, :, lanes] for ref in refs], axis=0)
        g_all = jnp.concatenate([ref[1, :, lanes] for ref in refs], axis=0)
        scores = near(dot(q_all, keys(0)))
        scores = jnp.concatenate([scores[: 2 * BAND], scores[2 * BAND :] + bias_ref[0]], axis=0)
        weights = jnp.exp(scores - column(0))
        store(1, dot(g_all.T, full(weights)))
        slopes = weights * (near(dot(g_all, keys(1))) - column(2))
        store(0, dot(q_all.T, full(slopes)))

    each_pair(own_ref.shape[-1], step)


def order_kernel(odd_ref, q_ref, g_ref, out_ref):
    odd = odd_ref[0] == 1
    out_ref[0] = (tile_order(q_ref[...].astype(F32), odd) * SCALE).astype(BF16)
    out_ref[1] = tile_order(g_ref[...].astype(F32), odd).astype(BF16)


def pack_kernel(odd_ref, own_ref, even_ref, odds_ref, first_ref, second_ref):
    odd = odd_ref[0] == 1
    for which in range(2):
        for band, ref in enumerate((own_ref, even_ref, odds_ref)):
            x = ref[which].astype(F32).reshape(TILE, 2 * TILE, ref.shape[-1])
            ordered = tile_order(x, odd).astype(BF16)
            first_ref[which, band * CELLS : (band + 1) * CELLS] = ordered[:CELLS]
            second_ref[which, band * CELLS : (band + 1) * CELLS] = ordered[CELLS:]


def finish_kernel(odd_ref, mid_ref, first_ref, second_ref, dk_ref, dv_ref):
    odd = odd_ref[0] == 1
    for which, out in ((0, dk_ref), (1, dv_ref)):
        sides = jnp.concatenate([first_ref[which], second_ref[which]], axis=0).astype(F32)
        mid = mid_ref[which].reshape(TILE, 2 * TILE, mid_ref.shape[-1])
        out[...] = (mid + grid_order(sides, odd)).astype(BF16)


def call(kernel, name, scalars, arrays, outs, flops, moved):
    return pl.pallas_call(
        kernel,
        in_specs=[pl.BlockSpec(memory_space=pltpu.SMEM)] * len(scalars)
        + [pl.BlockSpec(memory_space=pltpu.VMEM)] * len(arrays),
        out_specs=[pl.BlockSpec(memory_space=pltpu.VMEM)] * len(outs),
        out_shape=[jax.ShapeDtypeStruct(*out) for out in outs],
        compiler_params=pltpu.CompilerParams(vmem_limit_bytes=32 << 20),
        cost_estimate=pl.CostEstimate(flops=flops, bytes_accessed=moved, transcendentals=0),
        name=name,
    )(*scalars, *arrays)


def swap(value, axis, start, closed):
    count = lax.axis_size(axis)
    pairs = []
    for low in range(start, count if closed else count - 1, 2):
        high = (low + 1) % count
        pairs += [(low, high), (high, low)]
    return lax.ppermute(value, axis, pairs)


def shards(query_field, key_field, value_field, out_cotangent):
    band = lax.axis_index("lat")
    edge = (band == 0) | (band == lax.axis_size("lat") - 1)
    bias = jnp.where(edge, FAR, 0.0).astype(F32)[None]
    odd = (lax.axis_index("lon") % 2).astype(jnp.int32)[None]
    field, width = query_field.shape, query_field.shape[-1]
    pairs = width // PAIR
    keys = jnp.stack([key_field.reshape(BAND, width), value_field.reshape(BAND, width)])
    keys_even, keys_odd = swap(keys, "lat", 0, False), swap(keys, "lat", 1, False)
    (queries,) = call(
        order_kernel, "order", [odd], [query_field, out_cotangent], [((2, BAND, width), BF16)], 1 << 20, 1 << 20
    )
    queries_even, queries_odd = swap(queries, "lat", 0, False), swap(queries, "lat", 1, False)
    column = ((2, 3 * CELLS, width), BF16)
    first, second = call(
        pack_kernel, "pack", [odd], [keys, keys_even, keys_odd], [column, column], 1 << 20, 2 << 20
    )
    keys_first, keys_second = swap(first, "lon", 0, True), swap(second, "lon", 1, True)
    att, dq, stats = call(
        query_kernel, "queries", [bias, odd],
        [queries, keys, keys_even, keys_odd, keys_first, keys_second],
        [(field, BF16), (field, BF16), ((pairs, 8, PAIR), F32)], 1 << 31, 8 << 20,
    )
    stats_even, stats_odd = swap(stats, "lat", 0, False), swap(stats, "lat", 1, False)
    tile = ((2, CELLS, width), BF16)
    mid, first, second = call(
        key_kernel, "keys", [bias],
        [keys, keys_first, keys_second, queries, queries_even, queries_odd, stats, stats_even, stats_odd],
        [((2, BAND, width), F32), tile, tile], 1 << 31, 8 << 20,
    )
    from_first, from_second = swap(first, "lon", 0, True), swap(second, "lon", 1, True)
    dk, dv = call(
        finish_kernel, "finish", [odd], [mid, from_first, from_second], [(field, BF16), (field, BF16)], 1 << 20, 2 << 20
    )
    return att, dq, dk, dv


def solution(mesh):
    spec = P("lat", "lon", None)
    return jax.shard_map(
        shards, mesh=mesh, in_specs=(spec,) * 4, out_specs=(spec,) * 4, check_vma=False
    )
```

```python
import jax
import jax.numpy as jnp
from jax import lax
from jax.experimental import pallas as pl
from jax.experimental.pallas import tpu as pltpu
from jax.sharding import PartitionSpec as P


HEAD_DIM = 64
TILE = 8
CELLS = TILE * TILE
BAND = 2 * CELLS
PAIR = 2 * HEAD_DIM
SCALE = HEAD_DIM**-0.5
FAR = -1e30
F32, BF16 = jnp.float32, jnp.bfloat16
UNROLL = 6


def dot(a, b):
    return jnp.dot(a, b, preferred_element_type=F32)


def tile_order(x, odd):
    west = x[:, :TILE].reshape(CELLS, x.shape[-1])
    east = x[:, TILE:].reshape(CELLS, x.shape[-1])
    return jnp.concatenate([jnp.where(odd, west, east), jnp.where(odd, east, west)], axis=0)


def grid_order(x, odd):
    first = x[:CELLS].reshape(TILE, TILE, x.shape[-1])
    second = x[CELLS:].reshape(TILE, TILE, x.shape[-1])
    return jnp.concatenate([jnp.where(odd, first, second), jnp.where(odd, second, first)], axis=1)


def below(shape, axis, bound):
    return lax.broadcasted_iota(jnp.int32, shape, axis) < bound


def wide(x):
    row = below(x.shape, 0, HEAD_DIM)
    return jnp.concatenate([jnp.where(row, x, 0.0), jnp.where(row, 0.0, x)], axis=1).astype(BF16)


def diagonal(x):
    return jnp.concatenate([x[:HEAD_DIM, :PAIR], x[HEAD_DIM:, PAIR : 2 * PAIR]], axis=0)


def by_head(x):
    return jnp.concatenate(
        [
            jnp.sum(x[:HEAD_DIM], axis=0, keepdims=True),
            jnp.sum(x[HEAD_DIM:], axis=0, keepdims=True),
        ],
        axis=1,
    )


def each_pair(width, step):
    def body(p, carry):
        step(p, pl.ds(pl.multiple_of(p * PAIR, PAIR), PAIR))
        return carry

    lax.fori_loop(0, width // PAIR, body, 0, unroll=UNROLL)


CORE, SIDE = 3 * BAND, 3 * CELLS


def beside_first(rows):
    return (lax.broadcasted_iota(jnp.int32, (rows, 2 * PAIR), 1) & CELLS) == 0


def near(x):
    sides = jnp.where(beside_first(SIDE), x[CORE : CORE + SIDE], x[CORE + SIDE :])
    return jnp.concatenate([x[:CORE], sides], axis=0)


def split(x):
    first, none = beside_first(x.shape[0]), jnp.zeros((), x.dtype)
    return [jnp.where(first, x, none), jnp.where(first, none, x)]


def attend_kernel(
    bias_ref, odd_ref, mine_ref, own_ref, even_ref, odds_ref, first_ref, second_ref, att_ref, stats_ref, low_ref
):
    odd = odd_ref[0] == 1
    refs = (own_ref, even_ref, odds_ref, first_ref, second_ref)

    def step(p, lanes):
        k_all = jnp.concatenate([ref[0, :, lanes] for ref in refs], axis=0)
        v_all = jnp.concatenate([ref[1, :, lanes] for ref in refs], axis=0)
        q_turn = mine_ref[0, :, lanes].astype(F32).T
        g_turn = mine_ref[1, :, lanes].astype(F32).T
        scores = near(dot(k_all, wide(q_turn)))
        cut, last = 2 * BAND, CORE + 2 * CELLS
        bias = bias_ref[0]
        scores = jnp.concatenate(
            [scores[:cut], scores[cut:CORE] + bias, scores[CORE:last], scores[last:] + bias], axis=0
        )
        peak = jnp.max(scores, axis=0, keepdims=True)
        raised = jnp.exp(scores - peak)
        total = jnp.sum(raised, axis=0, keepdims=True)
        low = (raised * (1.0 / total)).astype(BF16)
        low_ref[p] = low
        full = jnp.concatenate([low[:CORE], *split(low[CORE:])], axis=0)
        att_turn = diagonal(dot(v_all.T, full)).astype(BF16).astype(F32)
        att_ref[:, :, lanes] = grid_order(att_turn.T, odd).astype(BF16)
        drift = by_head(g_turn * att_turn)
        log_total = peak + jnp.log(total)
        stats_ref[p] = jnp.concatenate(
            [log_total[:, :PAIR], log_total[:, PAIR:], drift[:, :PAIR], drift[:, PAIR:], jnp.zeros((4, PAIR), F32)],
            axis=0,
        )

    each_pair(mine_ref.shape[-1], step)


def slope_kernel(
    odd_ref, mine_ref, own_ref, even_ref, odds_ref, first_ref, second_ref, stats_ref, low_ref, dq_ref, part_ref
):
    odd = odd_ref[0] == 1
    refs = (own_ref, even_ref, odds_ref, first_ref, second_ref)

    def step(p, lanes):
        k_all = jnp.concatenate([ref[0, :, lanes] for ref in refs], axis=0)
        v_all = jnp.concatenate([ref[1, :, lanes] for ref in refs], axis=0)
        q_mine, g_mine = mine_ref[0, :, lanes], mine_ref[1, :, lanes]
        stats = stats_ref[p]
        drift = jnp.concatenate([stats[2:3], stats[3:4]], axis=1)
        low = low_ref[p]
        slopes = (low.astype(F32) * (near(dot(v_all, wide(g_mine.astype(F32).T))) - drift)).astype(BF16)
        full = jnp.concatenate([slopes[:CORE], *split(slopes[CORE:])], axis=0)
        dq_turn = diagonal(dot(k_all.T, full)) * SCALE
        dq_ref[:, :, lanes] = grid_order(dq_turn.T, odd).astype(BF16)
        lane = below((PAIR, PAIR), 1, HEAD_DIM)
        for which, rows, mine in ((0, slopes, q_mine), (1, low, g_mine)):
            none = jnp.zeros((), BF16)
            tall = jnp.concatenate([jnp.where(lane, mine, none), jnp.where(lane, none, mine)], axis=0)
            rows = jnp.concatenate([rows[:BAND], *split(rows[CORE : CORE + CELLS])], axis=0)
            part_ref[which, :, lanes] = dot(rows, tall)

    each_pair(mine_ref.shape[-1], step)


def key_kernel(
    bias_ref, own_ref, first_ref, second_ref, even_ref, odds_ref, even_stats, odds_stats, part_ref,
    mid_ref, to_first_ref, to_second_ref,
):
    refs = (even_ref, odds_ref)

    def step(p, lanes):
        low_lane = below((PAIR, PAIR), 1, CELLS)
        low_row = below((PAIR, PAIR), 0, HEAD_DIM)

        def keys(which):
            own = own_ref[which, :, lanes].astype(F32).T
            both = jnp.concatenate(
                [first_ref[which, :CELLS, lanes], second_ref[which, :CELLS, lanes]], axis=0
            ).astype(F32).T
            turned = pltpu.roll(both, CELLS, axis=1)
            block = low_row == low_lane
            first = jnp.where(block, jnp.where(low_lane, both, turned), 0.0).astype(BF16)
            second = jnp.where(block, jnp.where(low_lane, turned, both), 0.0).astype(BF16)
            return jnp.concatenate([wide(own), first, second], axis=1)

        def beside(x):
            sides = [
                x[at * CELLS : (at + 1) * CELLS, (2 + at % 2) * PAIR : (3 + at % 2) * PAIR] for at in range(4)
            ]
            return jnp.concatenate([x[:, : 2 * PAIR], jnp.concatenate(sides, axis=0)], axis=1)

        def spread(x):
            x = x.astype(BF16)
            none = jnp.zeros((CELLS, PAIR), BF16)
            sides = [x[at * CELLS : (at + 1) * CELLS, 2 * PAIR :] for at in range(4)]
            first = jnp.concatenate([none if at % 2 else sides[at] for at in range(4)], axis=0)
            second = jnp.concatenate([sides[at] if at % 2 else none for at in range(4)], axis=0)
            return jnp.concatenate([x[:, : 2 * PAIR], first, second], axis=1)

        stats = [ref[p] for ref in (even_stats, odds_stats)]
        columns = jnp.concatenate(stats + [jnp.zeros((PAIR - 16, PAIR), F32)], axis=0).T

        def column(base):
            rows = []
            for at in range(2):
                head0 = jnp.broadcast_to(columns[:, 8 * at + base : 8 * at + base + 1], (PAIR, PAIR))
                head1 = jnp.broadcast_to(columns[:, 8 * at + base + 1 : 8 * at + base + 2], (PAIR, PAIR))
                rows.append(jnp.concatenate([head0, head1, jnp.where(low_lane, head0, head1)], axis=1))
            return jnp.concatenate(rows, axis=0)

        def store(which, x):
            part = part_ref[which, :, lanes]
            mid_ref[which, :, lanes] = part[:BAND] + diagonal(x).T
            first, second = x[:, 2 * PAIR : 3 * PAIR], x[:, 3 * PAIR :]
            first = jnp.where(low_row, first, pltpu.roll(first, CELLS, axis=1))
            second = jnp.where(low_row, pltpu.roll(second, CELLS, axis=1), second)
            both = (part[BAND:] + jnp.where(low_lane, first, second).T).astype(BF16)
            to_first_ref[which, :, lanes] = both[:CELLS]
            to_second_ref[which, :, lanes] = both[CELLS:]

        q_all = jnp.concatenate([ref[0, :, lanes] for ref in refs], axis=0)
        g_all = jnp.concatenate([ref[1, :, lanes] for ref in refs], axis=0)
        scores = beside(dot(q_all, keys(0)))
        scores = jnp.concatenate([scores[:BAND], scores[BAND:] + bias_ref[0]], axis=0)
        weights = jnp.exp(scores - column(0))
        store(1, dot(g_all.T, spread(weights)))
        slopes = weights * (beside(dot(g_all, keys(1))) - column(2))
        store(0, dot(q_all.T, spread(slopes)))

    each_pair(own_ref.shape[-1], step)


def order_kernel(odd_ref, q_ref, g_ref, out_ref):
    odd = odd_ref[0] == 1
    out_ref[0] = (tile_order(q_ref[...].astype(F32), odd) * SCALE).astype(BF16)
    out_ref[1] = tile_order(g_ref[...].astype(F32), odd).astype(BF16)


def pack_kernel(odd_ref, own_ref, even_ref, odds_ref, first_ref, second_ref):
    odd = odd_ref[0] == 1
    for which in range(2):
        for band, ref in enumerate((own_ref, even_ref, odds_ref)):
            x = ref[which].astype(F32).reshape(TILE, 2 * TILE, ref.shape[-1])
            ordered = tile_order(x, odd).astype(BF16)
            first_ref[which, band * CELLS : (band + 1) * CELLS] = ordered[:CELLS]
            second_ref[which, band * CELLS : (band + 1) * CELLS] = ordered[CELLS:]


def finish_kernel(odd_ref, mid_ref, first_ref, second_ref, dk_ref, dv_ref):
    odd = odd_ref[0] == 1
    for which, out in ((0, dk_ref), (1, dv_ref)):
        sides = jnp.concatenate([first_ref[which], second_ref[which]], axis=0).astype(F32)
        mid = mid_ref[which].reshape(TILE, 2 * TILE, mid_ref.shape[-1])
        out[...] = (mid + grid_order(sides, odd)).astype(BF16)


def call(kernel, scalars, arrays, outs, flops, moved):
    return pl.pallas_call(
        kernel,
        in_specs=[pl.BlockSpec(memory_space=pltpu.SMEM)] * len(scalars)
        + [pl.BlockSpec(memory_space=pltpu.VMEM)] * len(arrays),
        out_specs=[pl.BlockSpec(memory_space=pltpu.VMEM)] * len(outs),
        out_shape=[jax.ShapeDtypeStruct(*out) for out in outs],
        compiler_params=pltpu.CompilerParams(vmem_limit_bytes=32 << 20),
        cost_estimate=pl.CostEstimate(flops=flops, bytes_accessed=moved, transcendentals=0),
    )(*scalars, *arrays)


def swap(value, axis, start, closed):
    count = lax.axis_size(axis)
    pairs = []
    for low in range(start, count if closed else count - 1, 2):
        high = (low + 1) % count
        pairs += [(low, high), (high, low)]
    return lax.ppermute(value, axis, pairs)


def block(query_field, key_field, value_field, out_cotangent):
    band = lax.axis_index("lat")
    edge = (band == 0) | (band == lax.axis_size("lat") - 1)
    bias = jnp.where(edge, FAR, 0.0).astype(F32)[None]
    odd = (lax.axis_index("lon") % 2).astype(jnp.int32)[None]
    field, width = query_field.shape, query_field.shape[-1]
    pairs = width // PAIR
    keys = jnp.stack([key_field.reshape(BAND, width), value_field.reshape(BAND, width)])
    keys_even = swap(keys, "lat", 0, False)
    keys_odd = swap(keys, "lat", 1, False)
    (queries,) = call(order_kernel, [odd], [query_field, out_cotangent], [((2, BAND, width), BF16)], 1 << 20, 1 << 20)
    queries_even = swap(queries, "lat", 0, False)
    queries_odd = swap(queries, "lat", 1, False)
    column = ((2, 3 * CELLS, width), BF16)
    first, second = call(pack_kernel, [odd], [keys, keys_even, keys_odd], [column, column], 1 << 20, 2 << 20)
    keys_second = swap(second, "lon", 1, True)
    keys_first = swap(first, "lon", 0, True)
    around = [queries, keys, keys_even, keys_odd, keys_first, keys_second]
    att, stats, low = call(
        attend_kernel, [bias, odd], around,
        [(field, BF16), ((pairs, 8, PAIR), F32), ((pairs, CORE + SIDE, 2 * PAIR), BF16)], 1 << 30, 8 << 20,
    )
    stats_odd = swap(stats, "lat", 1, False)
    stats_even = swap(stats, "lat", 0, False)
    dq, part = call(
        slope_kernel, [odd], [*around, stats, low],
        [(field, BF16), ((2, 2 * BAND, width), F32)], 1 << 30, 8 << 20,
    )
    tile = ((2, CELLS, width), BF16)
    mid, first, second = call(
        key_kernel, [bias],
        [keys, keys_first, keys_second, queries_even, queries_odd, stats_even, stats_odd, part],
        [((2, BAND, width), F32), tile, tile], 1 << 30, 8 << 20,
    )
    from_second = swap(second, "lon", 1, True)
    from_first = swap(first, "lon", 0, True)
    dk, dv = call(
        finish_kernel, [odd], [mid, from_first, from_second], [(field, BF16), (field, BF16)], 1 << 20, 2 << 20
    )
    return att, dq, dk, dv


def solution(mesh):
    spec = P("lat", "lon", None)
    return jax.shard_map(block, mesh=mesh, in_specs=(spec,) * 4, out_specs=(spec,) * 4, check_vma=False)
```

```python
import jax
import jax.numpy as jnp
from jax import lax
from jax.experimental import pallas as pl
from jax.experimental.pallas import tpu as pltpu
from jax.sharding import PartitionSpec as P


HEAD_DIM = 64
TILE = 8
CELLS = TILE * TILE
BAND = 2 * CELLS
PAIR = 2 * HEAD_DIM
SCALE = HEAD_DIM**-0.5
FAR = -1e30
F32, BF16 = jnp.float32, jnp.bfloat16
UNROLL = 6


def dot(a, b):
    return jnp.dot(a, b, preferred_element_type=F32)


def tile_order(x, odd):
    west = x[:, :TILE].reshape(CELLS, x.shape[-1])
    east = x[:, TILE:].reshape(CELLS, x.shape[-1])
    return jnp.concatenate([jnp.where(odd, west, east), jnp.where(odd, east, west)], axis=0)


def grid_order(x, odd):
    first = x[:CELLS].reshape(TILE, TILE, x.shape[-1])
    second = x[CELLS:].reshape(TILE, TILE, x.shape[-1])
    return jnp.concatenate([jnp.where(odd, first, second), jnp.where(odd, second, first)], axis=1)


def below(shape, axis, bound):
    return lax.broadcasted_iota(jnp.int32, shape, axis) < bound


def wide(x):
    row = below(x.shape, 0, HEAD_DIM)
    return jnp.concatenate([jnp.where(row, x, 0.0), jnp.where(row, 0.0, x)], axis=1).astype(BF16)


def diagonal(x):
    return jnp.concatenate([x[:HEAD_DIM, :PAIR], x[HEAD_DIM:, PAIR : 2 * PAIR]], axis=0)


def by_head(x):
    return jnp.concatenate(
        [
            jnp.sum(x[:HEAD_DIM], axis=0, keepdims=True),
            jnp.sum(x[HEAD_DIM:], axis=0, keepdims=True),
        ],
        axis=1,
    )


def each_pair(width, step):
    def body(p, carry):
        step(p, pl.ds(pl.multiple_of(p * PAIR, PAIR), PAIR))
        return carry

    lax.fori_loop(0, width // PAIR, body, 0, unroll=UNROLL)


CORE, SIDE = 3 * BAND, 3 * CELLS


def beside_first(rows):
    return (lax.broadcasted_iota(jnp.int32, (rows, 2 * PAIR), 1) & CELLS) == 0


def near(x):
    sides = jnp.where(beside_first(SIDE), x[CORE : CORE + SIDE], x[CORE + SIDE :])
    return jnp.concatenate([x[:CORE], sides], axis=0)


def split(x):
    first, none = beside_first(x.shape[0]), jnp.zeros((), x.dtype)
    return [jnp.where(first, x, none), jnp.where(first, none, x)]


def attend_kernel(
    bias_ref, odd_ref, mine_ref, own_ref, even_ref, odds_ref,
    first_ref, first_odds_ref, second_ref, second_odds_ref, att_ref, stats_ref, low_ref,
):
    odd = odd_ref[0] == 1
    refs = (own_ref, even_ref, odds_ref, first_ref, first_odds_ref, second_ref, second_odds_ref)

    def step(p, lanes):
        k_all = jnp.concatenate([ref[0, :, lanes] for ref in refs], axis=0)
        v_all = jnp.concatenate([ref[1, :, lanes] for ref in refs], axis=0)
        q_turn = mine_ref[0, :, lanes].astype(F32).T
        g_turn = mine_ref[1, :, lanes].astype(F32).T
        scores = near(dot(k_all, wide(q_turn)))
        cut, last = 2 * BAND, CORE + 2 * CELLS
        bias = bias_ref[0]
        scores = jnp.concatenate(
            [scores[:cut], scores[cut:CORE] + bias, scores[CORE:last], scores[last:] + bias], axis=0
        )
        peak = jnp.max(scores, axis=0, keepdims=True)
        raised = jnp.exp(scores - peak)
        total = jnp.sum(raised, axis=0, keepdims=True)
        low = (raised * (1.0 / total)).astype(BF16)
        low_ref[p] = low
        full = jnp.concatenate([low[:CORE], *split(low[CORE:])], axis=0)
        att_turn = diagonal(dot(v_all.T, full)).astype(BF16).astype(F32)
        att_ref[:, :, lanes] = grid_order(att_turn.T, odd).astype(BF16)
        drift = by_head(g_turn * att_turn)
        log_total = peak + jnp.log(total)
        stats_ref[p] = jnp.concatenate(
            [log_total[:, :PAIR], log_total[:, PAIR:], drift[:, :PAIR], drift[:, PAIR:], jnp.zeros((4, PAIR), F32)],
            axis=0,
        )

    each_pair(mine_ref.shape[-1], step)


def slope_kernel(
    odd_ref, mine_ref, own_ref, even_ref, odds_ref,
    first_ref, first_odds_ref, second_ref, second_odds_ref, stats_ref, low_ref, dq_ref, part_ref,
):
    odd = odd_ref[0] == 1
    refs = (own_ref, even_ref, odds_ref, first_ref, first_odds_ref, second_ref, second_odds_ref)

    def step(p, lanes):
        k_all = jnp.concatenate([ref[0, :, lanes] for ref in refs], axis=0)
        v_all = jnp.concatenate([ref[1, :, lanes] for ref in refs], axis=0)
        q_mine, g_mine = mine_ref[0, :, lanes], mine_ref[1, :, lanes]
        stats = stats_ref[p]
        drift = jnp.concatenate([stats[2:3], stats[3:4]], axis=1)
        low = low_ref[p]
        slopes = (low.astype(F32) * (near(dot(v_all, wide(g_mine.astype(F32).T))) - drift)).astype(BF16)
        full = jnp.concatenate([slopes[:CORE], *split(slopes[CORE:])], axis=0)
        dq_turn = diagonal(dot(k_all.T, full)) * SCALE
        dq_ref[:, :, lanes] = grid_order(dq_turn.T, odd).astype(BF16)
        lane = below((PAIR, PAIR), 1, HEAD_DIM)
        for which, rows, mine in ((0, slopes, q_mine), (1, low, g_mine)):
            none = jnp.zeros((), BF16)
            tall = jnp.concatenate([jnp.where(lane, mine, none), jnp.where(lane, none, mine)], axis=0)
            part_ref[which, :, lanes] = dot(rows[:BAND], tall)

    each_pair(mine_ref.shape[-1], step)


def stat_columns(refs, p):
    stats = [ref[p] for ref in refs]
    turned = jnp.concatenate(stats + [jnp.zeros((PAIR - 8 * len(refs), PAIR), F32)], axis=0).T

    def column(at, row):
        return jnp.broadcast_to(turned[:, 8 * at + row : 8 * at + row + 1], (PAIR, PAIR))

    return column


def side_kernel(
    bias_ref, first_ref, second_ref, mine_ref, even_ref, odds_ref, mine_stats, even_stats, odds_stats,
    to_first_ref, to_second_ref,
):
    refs = (mine_ref, even_ref, odds_ref)
    blocks = range(2 * len(refs))

    def step(p, lanes):
        low_lane = below((PAIR, PAIR), 1, CELLS)
        low_row = below((PAIR, PAIR), 0, HEAD_DIM)

        def keys(which):
            both = jnp.concatenate(
                [first_ref[which, :CELLS, lanes], second_ref[which, :CELLS, lanes]], axis=0
            ).astype(F32).T
            turned = pltpu.roll(both, CELLS, axis=1)
            block = low_row == low_lane
            first = jnp.where(block, jnp.where(low_lane, both, turned), 0.0)
            second = jnp.where(block, jnp.where(low_lane, turned, both), 0.0)
            return jnp.concatenate([first, second], axis=1).astype(BF16)

        def beside(x):
            return jnp.concatenate(
                [x[at * CELLS : (at + 1) * CELLS, at % 2 * PAIR : (1 + at % 2) * PAIR] for at in blocks], axis=0
            )

        def spread(x):
            x = x.astype(BF16)
            none = jnp.zeros((CELLS, PAIR), BF16)
            rows = [x[at * CELLS : (at + 1) * CELLS] for at in blocks]
            first = jnp.concatenate([none if at % 2 else rows[at] for at in blocks], axis=0)
            second = jnp.concatenate([rows[at] if at % 2 else none for at in blocks], axis=0)
            return jnp.concatenate([first, second], axis=1)

        def store(which, x):
            first, second = x[:, :PAIR], x[:, PAIR:]
            first = jnp.where(low_row, first, pltpu.roll(first, CELLS, axis=1))
            second = jnp.where(low_row, pltpu.roll(second, CELLS, axis=1), second)
            both = jnp.where(low_lane, first, second).T.astype(BF16)
            to_first_ref[which, :, lanes] = both[:CELLS]
            to_second_ref[which, :, lanes] = both[CELLS:]

        stat = stat_columns((mine_stats, even_stats, odds_stats), p)

        def column(base):
            return jnp.concatenate(
                [jnp.where(low_lane, stat(at, base), stat(at, base + 1)) for at in range(len(refs))], axis=0
            )

        q_all = jnp.concatenate([ref[0, :, lanes] for ref in refs], axis=0)
        g_all = jnp.concatenate([ref[1, :, lanes] for ref in refs], axis=0)
        scores = beside(dot(q_all, keys(0)))
        scores = jnp.concatenate([scores[: 2 * BAND], scores[2 * BAND :] + bias_ref[0]], axis=0)
        weights = jnp.exp(scores - column(0))
        store(1, dot(g_all.T, spread(weights)))
        slopes = weights * (beside(dot(g_all, keys(1))) - column(2))
        store(0, dot(q_all.T, spread(slopes)))

    each_pair(mine_ref.shape[-1], step)


def own_kernel(bias_ref, own_ref, even_ref, odds_ref, even_stats, odds_stats, part_ref, mid_ref):
    refs = (even_ref, odds_ref)

    def step(p, lanes):
        stat = stat_columns((even_stats, odds_stats), p)

        def column(base):
            return jnp.concatenate(
                [jnp.concatenate([stat(at, base), stat(at, base + 1)], axis=1) for at in range(len(refs))], axis=0
            )

        q_all = jnp.concatenate([ref[0, :, lanes] for ref in refs], axis=0)
        g_all = jnp.concatenate([ref[1, :, lanes] for ref in refs], axis=0)
        scores = dot(q_all, wide(own_ref[0, :, lanes].astype(F32).T))
        scores = jnp.concatenate([scores[:BAND], scores[BAND:] + bias_ref[0]], axis=0)
        weights = jnp.exp(scores - column(0))
        mid_ref[1, :, lanes] = part_ref[1, :, lanes] + diagonal(dot(g_all.T, weights.astype(BF16))).T
        products = dot(g_all, wide(own_ref[1, :, lanes].astype(F32).T))
        slopes = (weights * (products - column(2))).astype(BF16)
        mid_ref[0, :, lanes] = part_ref[0, :, lanes] + diagonal(dot(q_all.T, slopes)).T

    each_pair(own_ref.shape[-1], step)


def order_kernel(odd_ref, q_ref, g_ref, out_ref):
    odd = odd_ref[0] == 1
    out_ref[0] = (tile_order(q_ref[...].astype(F32), odd) * SCALE).astype(BF16)
    out_ref[1] = tile_order(g_ref[...].astype(F32), odd).astype(BF16)


def pack_kernel(odd_ref, *refs):
    odd = odd_ref[0] == 1
    bands, (first_ref, second_ref) = refs[:-2], refs[-2:]
    for which in range(2):
        for at, ref in enumerate(bands):
            x = ref[which].astype(F32).reshape(TILE, 2 * TILE, ref.shape[-1])
            ordered = tile_order(x, odd).astype(BF16)
            first_ref[which, at * CELLS : (at + 1) * CELLS] = ordered[:CELLS]
            second_ref[which, at * CELLS : (at + 1) * CELLS] = ordered[CELLS:]


def finish_kernel(odd_ref, mid_ref, first_ref, second_ref, dk_ref, dv_ref):
    odd = odd_ref[0] == 1
    for which, out in ((0, dk_ref), (1, dv_ref)):
        sides = jnp.concatenate([first_ref[which], second_ref[which]], axis=0).astype(F32)
        mid = mid_ref[which].reshape(TILE, 2 * TILE, mid_ref.shape[-1])
        out[...] = (mid + grid_order(sides, odd)).astype(BF16)


def call(kernel, scalars, arrays, outs, flops, moved):
    return pl.pallas_call(
        kernel,
        in_specs=[pl.BlockSpec(memory_space=pltpu.SMEM)] * len(scalars)
        + [pl.BlockSpec(memory_space=pltpu.VMEM)] * len(arrays),
        out_specs=[pl.BlockSpec(memory_space=pltpu.VMEM)] * len(outs),
        out_shape=[jax.ShapeDtypeStruct(*out) for out in outs],
        compiler_params=pltpu.CompilerParams(vmem_limit_bytes=32 << 20),
        cost_estimate=pl.CostEstimate(flops=flops, bytes_accessed=moved, transcendentals=0),
    )(*scalars, *arrays)


def swap(value, axis, start, closed):
    count = lax.axis_size(axis)
    pairs = []
    for low in range(start, count if closed else count - 1, 2):
        high = (low + 1) % count
        pairs += [(low, high), (high, low)]
    return lax.ppermute(value, axis, pairs)


def block(query_field, key_field, value_field, out_cotangent):
    band = lax.axis_index("lat")
    edge = (band == 0) | (band == lax.axis_size("lat") - 1)
    bias = jnp.where(edge, FAR, 0.0).astype(F32)[None]
    odd = (lax.axis_index("lon") % 2).astype(jnp.int32)[None]
    field, width = query_field.shape, query_field.shape[-1]
    pairs = width // PAIR

    def named_swap(first, second, axis):
        second = swap(second, axis, 1, axis == "lon")
        first = swap(first, axis, 0, axis == "lon")
        return first, second

    def pack(*bands):
        column = ((2, len(bands) * CELLS, width), BF16)
        return call(pack_kernel, [odd], list(bands), [column, column], 1 << 20, 2 << 20)

    keys = jnp.stack([key_field.reshape(BAND, width), value_field.reshape(BAND, width)])
    keys_even, keys_odd = named_swap(keys, keys, "lat")
    first, second = named_swap(*pack(keys, keys_even), "lon")
    (queries,) = call(order_kernel, [odd], [query_field, out_cotangent], [((2, BAND, width), BF16)], 1 << 20, 1 << 20)
    queries_even, queries_odd = named_swap(queries, queries, "lat")
    first_odds, second_odds = named_swap(*pack(keys_odd), "lon")
    around = [queries, keys, keys_even, keys_odd, first, first_odds, second, second_odds]
    att, stats, low = call(
        attend_kernel, [bias, odd], around,
        [(field, BF16), ((pairs, 8, PAIR), F32), ((pairs, CORE + SIDE, 2 * PAIR), BF16)], 1 << 30, 8 << 20,
    )
    stats_even, stats_odd = named_swap(stats, stats, "lat")
    tile = ((2, CELLS, width), BF16)
    to_first, to_second = call(
        side_kernel, [bias],
        [first, second, queries, queries_even, queries_odd, stats, stats_even, stats_odd], [tile, tile],
        1 << 29, 4 << 20,
    )
    from_first, from_second = named_swap(to_first, to_second, "lon")
    dq, part = call(
        slope_kernel, [odd], [*around, stats, low],
        [(field, BF16), ((2, BAND, width), F32)], 1 << 30, 8 << 20,
    )
    (mid,) = call(
        own_kernel, [bias],
        [keys, queries_even, queries_odd, stats_even, stats_odd, part], [((2, BAND, width), F32)], 1 << 29, 4 << 20,
    )
    dk, dv = call(
        finish_kernel, [odd], [mid, from_first, from_second], [(field, BF16), (field, BF16)], 1 << 20, 2 << 20
    )
    return att, dq, dk, dv


def solution(mesh):
    spec = P("lat", "lon", None)
    return jax.shard_map(block, mesh=mesh, in_specs=(spec,) * 4, out_specs=(spec,) * 4, check_vma=False)
```

```python
import jax
import jax.numpy as jnp
from jax import lax
from jax.experimental import pallas as pl
from jax.experimental.pallas import tpu as pltpu
from jax.sharding import PartitionSpec as P


HEAD_DIM = 64
TILE = 8
CELLS = TILE * TILE
BAND = 2 * CELLS
PAIR = 2 * HEAD_DIM
SCALE = HEAD_DIM**-0.5
FAR = -1e30
F32, BF16 = jnp.float32, jnp.bfloat16
UNROLL = 6


def dot(a, b):
    return jnp.dot(a, b, preferred_element_type=F32)


def tile_order(x, odd):
    west = x[:, :TILE].reshape(CELLS, x.shape[-1])
    east = x[:, TILE:].reshape(CELLS, x.shape[-1])
    return jnp.concatenate([jnp.where(odd, west, east), jnp.where(odd, east, west)], axis=0)


def grid_order(x, odd):
    first = x[:CELLS].reshape(TILE, TILE, x.shape[-1])
    second = x[CELLS:].reshape(TILE, TILE, x.shape[-1])
    return jnp.concatenate([jnp.where(odd, first, second), jnp.where(odd, second, first)], axis=1)


def below(shape, axis, bound):
    return lax.broadcasted_iota(jnp.int32, shape, axis) < bound


def wide(x):
    row = below(x.shape, 0, HEAD_DIM)
    return jnp.concatenate([jnp.where(row, x, 0.0), jnp.where(row, 0.0, x)], axis=1).astype(BF16)


def diagonal(x):
    return jnp.concatenate([x[:HEAD_DIM, :PAIR], x[HEAD_DIM:, PAIR : 2 * PAIR]], axis=0)


def by_head(x):
    return jnp.concatenate(
        [
            jnp.sum(x[:HEAD_DIM], axis=0, keepdims=True),
            jnp.sum(x[HEAD_DIM:], axis=0, keepdims=True),
        ],
        axis=1,
    )


def each_pair(width, step):
    def body(p, carry):
        step(p, pl.ds(pl.multiple_of(p * PAIR, PAIR), PAIR))
        return carry

    lax.fori_loop(0, width // PAIR, body, 0, unroll=UNROLL)


CORE, SIDE = 3 * BAND, 3 * CELLS


def beside_first(rows):
    return (lax.broadcasted_iota(jnp.int32, (rows, 2 * PAIR), 1) & CELLS) == 0


def near(x):
    sides = jnp.where(beside_first(SIDE), x[CORE : CORE + SIDE], x[CORE + SIDE :])
    return jnp.concatenate([x[:CORE], sides], axis=0)


def split(x):
    first, none = beside_first(x.shape[0]), jnp.zeros((), x.dtype)
    return [jnp.where(first, x, none), jnp.where(first, none, x)]


def attend_kernel(
    bias_ref, odd_ref, mine_ref, own_ref, even_ref, odds_ref, first_ref, second_ref, att_ref, stats_ref, low_ref
):
    odd = odd_ref[0] == 1
    refs = (own_ref, even_ref, odds_ref, first_ref, second_ref)

    def step(p, lanes):
        k_all = jnp.concatenate([ref[0, :, lanes] for ref in refs], axis=0)
        v_all = jnp.concatenate([ref[1, :, lanes] for ref in refs], axis=0)
        q_turn = mine_ref[0, :, lanes].astype(F32).T
        g_turn = mine_ref[1, :, lanes].astype(F32).T
        scores = near(dot(k_all, wide(q_turn)))
        cut, last = 2 * BAND, CORE + 2 * CELLS
        bias = bias_ref[0]
        scores = jnp.concatenate(
            [scores[:cut], scores[cut:CORE] + bias, scores[CORE:last], scores[last:] + bias], axis=0
        )
        peak = jnp.max(scores, axis=0, keepdims=True)
        raised = jnp.exp(scores - peak)
        total = jnp.sum(raised, axis=0, keepdims=True)
        low = (raised * (1.0 / total)).astype(BF16)
        low_ref[p] = low
        full = jnp.concatenate([low[:CORE], *split(low[CORE:])], axis=0)
        att_turn = diagonal(dot(v_all.T, full)).astype(BF16).astype(F32)
        att_ref[:, :, lanes] = grid_order(att_turn.T, odd).astype(BF16)
        drift = by_head(g_turn * att_turn)
        log_total = peak + jnp.log(total)
        stats_ref[p] = jnp.concatenate(
            [log_total[:, :PAIR], log_total[:, PAIR:], drift[:, :PAIR], drift[:, PAIR:], jnp.zeros((4, PAIR), F32)],
            axis=0,
        )

    each_pair(mine_ref.shape[-1], step)


def slope_kernel(
    odd_ref, mine_ref, own_ref, even_ref, odds_ref, first_ref, second_ref, stats_ref, low_ref, dq_ref, part_ref
):
    odd = odd_ref[0] == 1
    refs = (own_ref, even_ref, odds_ref, first_ref, second_ref)

    def step(p, lanes):
        k_all = jnp.concatenate([ref[0, :, lanes] for ref in refs], axis=0)
        v_all = jnp.concatenate([ref[1, :, lanes] for ref in refs], axis=0)
        q_mine, g_mine = mine_ref[0, :, lanes], mine_ref[1, :, lanes]
        stats = stats_ref[p]
        drift = jnp.concatenate([stats[2:3], stats[3:4]], axis=1)
        low = low_ref[p]
        slopes = (low.astype(F32) * (near(dot(v_all, wide(g_mine.astype(F32).T))) - drift)).astype(BF16)
        full = jnp.concatenate([slopes[:CORE], *split(slopes[CORE:])], axis=0)
        dq_turn = diagonal(dot(k_all.T, full)) * SCALE
        dq_ref[:, :, lanes] = grid_order(dq_turn.T, odd).astype(BF16)
        lane = below((PAIR, PAIR), 1, HEAD_DIM)
        for which, rows, mine in ((0, slopes, q_mine), (1, low, g_mine)):
            none = jnp.zeros((), BF16)
            tall = jnp.concatenate([jnp.where(lane, mine, none), jnp.where(lane, none, mine)], axis=0)
            rows = jnp.concatenate([rows[:BAND], *split(rows[CORE : CORE + CELLS])], axis=0)
            part_ref[which, :, lanes] = dot(rows, tall)

    each_pair(mine_ref.shape[-1], step)


def key_kernel(
    bias_ref, own_ref, first_ref, second_ref, even_ref, odds_ref, even_stats, odds_stats, part_ref,
    mid_ref, to_first_ref, to_second_ref,
):
    refs = (even_ref, odds_ref)

    def step(p, lanes):
        low_lane = below((PAIR, PAIR), 1, CELLS)
        low_row = below((PAIR, PAIR), 0, HEAD_DIM)

        def keys(which):
            own = own_ref[which, :, lanes].astype(F32).T
            both = jnp.concatenate(
                [first_ref[which, :CELLS, lanes], second_ref[which, :CELLS, lanes]], axis=0
            ).astype(F32).T
            turned = pltpu.roll(both, CELLS, axis=1)
            block = low_row == low_lane
            first = jnp.where(block, jnp.where(low_lane, both, turned), 0.0).astype(BF16)
            second = jnp.where(block, jnp.where(low_lane, turned, both), 0.0).astype(BF16)
            return jnp.concatenate([wide(own), first, second], axis=1)

        def beside(x):
            sides = [
                x[at * CELLS : (at + 1) * CELLS, (2 + at % 2) * PAIR : (3 + at % 2) * PAIR] for at in range(4)
            ]
            return jnp.concatenate([x[:, : 2 * PAIR], jnp.concatenate(sides, axis=0)], axis=1)

        def spread(x):
            x = x.astype(BF16)
            none = jnp.zeros((CELLS, PAIR), BF16)
            sides = [x[at * CELLS : (at + 1) * CELLS, 2 * PAIR :] for at in range(4)]
            first = jnp.concatenate([none if at % 2 else sides[at] for at in range(4)], axis=0)
            second = jnp.concatenate([sides[at] if at % 2 else none for at in range(4)], axis=0)
            return jnp.concatenate([x[:, : 2 * PAIR], first, second], axis=1)

        stats = [ref[p] for ref in (even_stats, odds_stats)]
        columns = jnp.concatenate(stats + [jnp.zeros((PAIR - 16, PAIR), F32)], axis=0).T

        def column(base):
            rows = []
            for at in range(2):
                head0 = jnp.broadcast_to(columns[:, 8 * at + base : 8 * at + base + 1], (PAIR, PAIR))
                head1 = jnp.broadcast_to(columns[:, 8 * at + base + 1 : 8 * at + base + 2], (PAIR, PAIR))
                rows.append(jnp.concatenate([head0, head1, jnp.where(low_lane, head0, head1)], axis=1))
            return jnp.concatenate(rows, axis=0)

        def store(which, x):
            part = part_ref[which, :, lanes]
            mid_ref[which, :, lanes] = part[:BAND] + diagonal(x).T
            first, second = x[:, 2 * PAIR : 3 * PAIR], x[:, 3 * PAIR :]
            first = jnp.where(low_row, first, pltpu.roll(first, CELLS, axis=1))
            second = jnp.where(low_row, pltpu.roll(second, CELLS, axis=1), second)
            both = (part[BAND:] + jnp.where(low_lane, first, second).T).astype(BF16)
            to_first_ref[which, :, lanes] = both[:CELLS]
            to_second_ref[which, :, lanes] = both[CELLS:]

        q_all = jnp.concatenate([ref[0, :, lanes] for ref in refs], axis=0)
        g_all = jnp.concatenate([ref[1, :, lanes] for ref in refs], axis=0)
        scores = beside(dot(q_all, keys(0)))
        scores = jnp.concatenate([scores[:BAND], scores[BAND:] + bias_ref[0]], axis=0)
        weights = jnp.exp(scores - column(0))
        store(1, dot(g_all.T, spread(weights)))
        slopes = weights * (beside(dot(g_all, keys(1))) - column(2))
        store(0, dot(q_all.T, spread(slopes)))

    each_pair(own_ref.shape[-1], step)


def order_kernel(odd_ref, q_ref, g_ref, out_ref):
    odd = odd_ref[0] == 1
    out_ref[0] = (tile_order(q_ref[...].astype(F32), odd) * SCALE).astype(BF16)
    out_ref[1] = tile_order(g_ref[...].astype(F32), odd).astype(BF16)


def pack_kernel(odd_ref, *refs):
    odd = odd_ref[0] == 1
    bands, (first_ref, second_ref) = refs[:-2], refs[-2:]
    for which in range(2):
        for at, ref in enumerate(bands):
            x = ref[which].astype(F32).reshape(TILE, 2 * TILE, ref.shape[-1])
            ordered = tile_order(x, odd).astype(BF16)
            first_ref[which, at * CELLS : (at + 1) * CELLS] = ordered[:CELLS]
            second_ref[which, at * CELLS : (at + 1) * CELLS] = ordered[CELLS:]


def finish_kernel(odd_ref, mid_ref, first_ref, second_ref, dk_ref, dv_ref):
    odd = odd_ref[0] == 1
    for which, out in ((0, dk_ref), (1, dv_ref)):
        sides = jnp.concatenate([first_ref[which], second_ref[which]], axis=0).astype(F32)
        mid = mid_ref[which].reshape(TILE, 2 * TILE, mid_ref.shape[-1])
        out[...] = (mid + grid_order(sides, odd)).astype(BF16)


def call(kernel, scalars, arrays, outs, flops, moved):
    return pl.pallas_call(
        kernel,
        in_specs=[pl.BlockSpec(memory_space=pltpu.SMEM)] * len(scalars)
        + [pl.BlockSpec(memory_space=pltpu.VMEM)] * len(arrays),
        out_specs=[pl.BlockSpec(memory_space=pltpu.VMEM)] * len(outs),
        out_shape=[jax.ShapeDtypeStruct(*out) for out in outs],
        compiler_params=pltpu.CompilerParams(vmem_limit_bytes=20 << 20),
        cost_estimate=pl.CostEstimate(flops=flops, bytes_accessed=moved, transcendentals=0),
    )(*scalars, *arrays)


def swap(value, axis, start, closed):
    count = lax.axis_size(axis)
    pairs = []
    for low in range(start, count if closed else count - 1, 2):
        high = (low + 1) % count
        pairs += [(low, high), (high, low)]
    return lax.ppermute(value, axis, pairs)


def block(query_field, key_field, value_field, out_cotangent):
    band = lax.axis_index("lat")
    edge = (band == 0) | (band == lax.axis_size("lat") - 1)
    bias = jnp.where(edge, FAR, 0.0).astype(F32)[None]
    odd = (lax.axis_index("lon") % 2).astype(jnp.int32)[None]
    field, width = query_field.shape, query_field.shape[-1]
    pairs = width // PAIR

    def named_swap(first, second, axis):
        second = swap(second, axis, 1, axis == "lon")
        first = swap(first, axis, 0, axis == "lon")
        return first, second

    def pack(*bands):
        column = ((2, len(bands) * CELLS, width), BF16)
        return call(pack_kernel, [odd], list(bands), [column, column], 1 << 20, 2 << 20)

    keys = jnp.stack([key_field.reshape(BAND, width), value_field.reshape(BAND, width)])
    keys_even, keys_odd = named_swap(keys, keys, "lat")
    (queries,) = call(order_kernel, [odd], [query_field, out_cotangent], [((2, BAND, width), BF16)], 1 << 20, 1 << 20)
    queries_even, queries_odd = named_swap(queries, queries, "lat")
    first, second = named_swap(*pack(keys, keys_even, keys_odd), "lon")
    around = [queries, keys, keys_even, keys_odd, first, second]
    att, stats, low = call(
        attend_kernel, [bias, odd], around,
        [(field, BF16), ((pairs, 8, PAIR), F32), ((pairs, CORE + SIDE, 2 * PAIR), BF16)], 1 << 30, 8 << 20,
    )
    stats_even, stats_odd = named_swap(stats, stats, "lat")
    dq, part = call(
        slope_kernel, [odd], [*around, stats, low],
        [(field, BF16), ((2, 2 * BAND, width), F32)], 1 << 30, 8 << 20,
    )
    tile = ((2, CELLS, width), BF16)
    mid, to_first, to_second = call(
        key_kernel, [bias],
        [keys, first, second, queries_even, queries_odd, stats_even, stats_odd, part],
        [((2, BAND, width), F32), tile, tile], 1 << 30, 8 << 20,
    )
    from_first, from_second = named_swap(to_first, to_second, "lon")
    dk, dv = call(
        finish_kernel, [odd], [mid, from_first, from_second], [(field, BF16), (field, BF16)], 1 << 20, 2 << 20
    )
    return att, dq, dk, dv


def solution(mesh):
    spec = P("lat", "lon", None)
    return jax.shard_map(block, mesh=mesh, in_specs=(spec,) * 4, out_specs=(spec,) * 4, check_vma=False)
```

```python
import jax
import jax.numpy as jnp
from jax import lax
from jax.experimental import pallas as pl
from jax.experimental.pallas import tpu as pltpu
from jax.sharding import PartitionSpec as P


HEAD_DIM = 64
TILE = 8
CELLS = TILE * TILE
BAND = 2 * CELLS
PAIR = 2 * HEAD_DIM
SCALE = HEAD_DIM**-0.5
FAR = -1e30
F32, BF16 = jnp.float32, jnp.bfloat16
UNROLL = 6


def dot(a, b):
    return jnp.dot(a, b, preferred_element_type=F32)


def tile_order(x, odd):
    west = x[:, :TILE].reshape(CELLS, x.shape[-1])
    east = x[:, TILE:].reshape(CELLS, x.shape[-1])
    return jnp.concatenate([jnp.where(odd, west, east), jnp.where(odd, east, west)], axis=0)


def grid_order(x, odd):
    first = x[:CELLS].reshape(TILE, TILE, x.shape[-1])
    second = x[CELLS:].reshape(TILE, TILE, x.shape[-1])
    return jnp.concatenate([jnp.where(odd, first, second), jnp.where(odd, second, first)], axis=1)


def below(shape, axis, bound):
    return lax.broadcasted_iota(jnp.int32, shape, axis) < bound


def wide(x):
    row = below(x.shape, 0, HEAD_DIM)
    return jnp.concatenate([jnp.where(row, x, 0.0), jnp.where(row, 0.0, x)], axis=1).astype(BF16)


def diagonal(x):
    return jnp.concatenate([x[:HEAD_DIM, :PAIR], x[HEAD_DIM:, PAIR : 2 * PAIR]], axis=0)


def by_head(x):
    return jnp.concatenate(
        [
            jnp.sum(x[:HEAD_DIM], axis=0, keepdims=True),
            jnp.sum(x[HEAD_DIM:], axis=0, keepdims=True),
        ],
        axis=1,
    )


def each_pair(width, step):
    def body(p, carry):
        step(p, pl.ds(pl.multiple_of(p * PAIR, PAIR), PAIR))
        return carry

    lax.fori_loop(0, width // PAIR, body, 0, unroll=UNROLL)


CORE, SIDE = 3 * BAND, 3 * CELLS


def beside_first(rows):
    return (lax.broadcasted_iota(jnp.int32, (rows, 2 * PAIR), 1) & CELLS) == 0


def near(x):
    sides = jnp.where(beside_first(SIDE), x[CORE : CORE + SIDE], x[CORE + SIDE :])
    return jnp.concatenate([x[:CORE], sides], axis=0)


def split(x):
    first, none = beside_first(x.shape[0]), jnp.zeros((), x.dtype)
    return [jnp.where(first, x, none), jnp.where(first, none, x)]


def attend_kernel(bias_ref, odd_ref, mine_ref, *refs):
    odd = odd_ref[0] == 1
    k_refs, v_refs, (att_ref, stats_ref, low_ref) = refs[:5], refs[5:10], refs[10:]

    def step(p, lanes):
        k_all = jnp.concatenate([ref[:, lanes] for ref in k_refs], axis=0)
        v_all = jnp.concatenate([ref[:, lanes] for ref in v_refs], axis=0)
        q_turn = mine_ref[0, :, lanes].astype(F32).T
        g_turn = mine_ref[1, :, lanes].astype(F32).T
        scores = near(dot(k_all, wide(q_turn)))
        cut, last = 2 * BAND, CORE + 2 * CELLS
        bias = bias_ref[0]
        scores = jnp.concatenate(
            [scores[:cut], scores[cut:CORE] + bias, scores[CORE:last], scores[last:] + bias], axis=0
        )
        peak = jnp.max(scores, axis=0, keepdims=True)
        raised = jnp.exp(scores - peak)
        total = jnp.sum(raised, axis=0, keepdims=True)
        low = (raised * (1.0 / total)).astype(BF16)
        low_ref[p] = low
        full = jnp.concatenate([low[:CORE], *split(low[CORE:])], axis=0)
        att_turn = diagonal(dot(v_all.T, full)).astype(BF16).astype(F32)
        att_ref[:, :, lanes] = grid_order(att_turn.T, odd).astype(BF16)
        drift = by_head(g_turn * att_turn)
        log_total = peak + jnp.log(total)
        stats_ref[p] = jnp.concatenate(
            [log_total[:, :PAIR], log_total[:, PAIR:], drift[:, :PAIR], drift[:, PAIR:], jnp.zeros((4, PAIR), F32)],
            axis=0,
        )

    each_pair(mine_ref.shape[-1], step)


def slope_kernel(odd_ref, mine_ref, *refs):
    odd = odd_ref[0] == 1
    k_refs, v_refs, (stats_ref, low_ref, dq_ref, part_ref) = refs[:5], refs[5:10], refs[10:]

    def step(p, lanes):
        k_all = jnp.concatenate([ref[:, lanes] for ref in k_refs], axis=0)
        v_all = jnp.concatenate([ref[:, lanes] for ref in v_refs], axis=0)
        q_mine, g_mine = mine_ref[0, :, lanes], mine_ref[1, :, lanes]
        stats = stats_ref[p]
        drift = jnp.concatenate([stats[2:3], stats[3:4]], axis=1)
        low = low_ref[p]
        slopes = (low.astype(F32) * (near(dot(v_all, wide(g_mine.astype(F32).T))) - drift)).astype(BF16)
        full = jnp.concatenate([slopes[:CORE], *split(slopes[CORE:])], axis=0)
        dq_turn = diagonal(dot(k_all.T, full)) * SCALE
        dq_ref[:, :, lanes] = grid_order(dq_turn.T, odd).astype(BF16)
        lane = below((PAIR, PAIR), 1, HEAD_DIM)
        for which, rows, mine in ((0, slopes, q_mine), (1, low, g_mine)):
            none = jnp.zeros((), BF16)
            tall = jnp.concatenate([jnp.where(lane, mine, none), jnp.where(lane, none, mine)], axis=0)
            rows = jnp.concatenate([rows[:BAND], *split(rows[CORE : CORE + CELLS])], axis=0)
            part_ref[which, :, lanes] = dot(rows, tall)

    each_pair(mine_ref.shape[-1], step)


def key_kernel(
    bias_ref, own_k_ref, first_k_ref, second_k_ref, own_v_ref, first_v_ref, second_v_ref,
    even_ref, odds_ref, even_stats, odds_stats, part_ref, mid_ref, to_first_ref, to_second_ref,
):
    own_refs, first_refs, second_refs = (own_k_ref, own_v_ref), (first_k_ref, first_v_ref), (second_k_ref, second_v_ref)
    refs = (even_ref, odds_ref)

    def step(p, lanes):
        low_lane = below((PAIR, PAIR), 1, CELLS)
        low_row = below((PAIR, PAIR), 0, HEAD_DIM)

        def keys(which):
            own = own_refs[which][:, lanes].astype(F32).T
            both = jnp.concatenate(
                [first_refs[which][:CELLS, lanes], second_refs[which][:CELLS, lanes]], axis=0
            ).astype(F32).T
            turned = pltpu.roll(both, CELLS, axis=1)
            block = low_row == low_lane
            first = jnp.where(block, jnp.where(low_lane, both, turned), 0.0).astype(BF16)
            second = jnp.where(block, jnp.where(low_lane, turned, both), 0.0).astype(BF16)
            return jnp.concatenate([wide(own), first, second], axis=1)

        def beside(x):
            sides = [
                x[at * CELLS : (at + 1) * CELLS, (2 + at % 2) * PAIR : (3 + at % 2) * PAIR] for at in range(4)
            ]
            return jnp.concatenate([x[:, : 2 * PAIR], jnp.concatenate(sides, axis=0)], axis=1)

        def spread(x):
            x = x.astype(BF16)
            none = jnp.zeros((CELLS, PAIR), BF16)
            sides = [x[at * CELLS : (at + 1) * CELLS, 2 * PAIR :] for at in range(4)]
            first = jnp.concatenate([none if at % 2 else sides[at] for at in range(4)], axis=0)
            second = jnp.concatenate([sides[at] if at % 2 else none for at in range(4)], axis=0)
            return jnp.concatenate([x[:, : 2 * PAIR], first, second], axis=1)

        stats = [ref[p] for ref in (even_stats, odds_stats)]
        columns = jnp.concatenate(stats + [jnp.zeros((PAIR - 16, PAIR), F32)], axis=0).T

        def column(base):
            rows = []
            for at in range(2):
                head0 = jnp.broadcast_to(columns[:, 8 * at + base : 8 * at + base + 1], (PAIR, PAIR))
                head1 = jnp.broadcast_to(columns[:, 8 * at + base + 1 : 8 * at + base + 2], (PAIR, PAIR))
                rows.append(jnp.concatenate([head0, head1, jnp.where(low_lane, head0, head1)], axis=1))
            return jnp.concatenate(rows, axis=0)

        def store(which, x):
            part = part_ref[which, :, lanes]
            mid_ref[which, :, lanes] = part[:BAND] + diagonal(x).T
            first, second = x[:, 2 * PAIR : 3 * PAIR], x[:, 3 * PAIR :]
            first = jnp.where(low_row, first, pltpu.roll(first, CELLS, axis=1))
            second = jnp.where(low_row, pltpu.roll(second, CELLS, axis=1), second)
            both = (part[BAND:] + jnp.where(low_lane, first, second).T).astype(BF16)
            to_first_ref[which, :, lanes] = both[:CELLS]
            to_second_ref[which, :, lanes] = both[CELLS:]

        q_all = jnp.concatenate([ref[0, :, lanes] for ref in refs], axis=0)
        g_all = jnp.concatenate([ref[1, :, lanes] for ref in refs], axis=0)
        scores = beside(dot(q_all, keys(0)))
        scores = jnp.concatenate([scores[:BAND], scores[BAND:] + bias_ref[0]], axis=0)
        weights = jnp.exp(scores - column(0))
        store(1, dot(g_all.T, spread(weights)))
        slopes = weights * (beside(dot(g_all, keys(1))) - column(2))
        store(0, dot(q_all.T, spread(slopes)))

    each_pair(own_k_ref.shape[-1], step)


def order_kernel(odd_ref, q_ref, g_ref, out_ref):
    odd = odd_ref[0] == 1
    out_ref[0] = (tile_order(q_ref[...].astype(F32), odd) * SCALE).astype(BF16)
    out_ref[1] = tile_order(g_ref[...].astype(F32), odd).astype(BF16)


def pack_kernel(odd_ref, *refs):
    odd = odd_ref[0] == 1
    bands, (first_ref, second_ref) = refs[:-2], refs[-2:]
    for at, ref in enumerate(bands):
        x = ref[...].astype(F32).reshape(TILE, 2 * TILE, ref.shape[-1])
        ordered = tile_order(x, odd).astype(BF16)
        first_ref[at * CELLS : (at + 1) * CELLS] = ordered[:CELLS]
        second_ref[at * CELLS : (at + 1) * CELLS] = ordered[CELLS:]


def finish_kernel(odd_ref, mid_ref, first_ref, second_ref, dk_ref, dv_ref):
    odd = odd_ref[0] == 1
    for which, out in ((0, dk_ref), (1, dv_ref)):
        sides = jnp.concatenate([first_ref[which], second_ref[which]], axis=0).astype(F32)
        mid = mid_ref[which].reshape(TILE, 2 * TILE, mid_ref.shape[-1])
        out[...] = (mid + grid_order(sides, odd)).astype(BF16)


def call(kernel, scalars, arrays, outs, flops, moved):
    return pl.pallas_call(
        kernel,
        in_specs=[pl.BlockSpec(memory_space=pltpu.SMEM)] * len(scalars)
        + [pl.BlockSpec(memory_space=pltpu.VMEM)] * len(arrays),
        out_specs=[pl.BlockSpec(memory_space=pltpu.VMEM)] * len(outs),
        out_shape=[jax.ShapeDtypeStruct(*out) for out in outs],
        compiler_params=pltpu.CompilerParams(vmem_limit_bytes=20 << 20),
        cost_estimate=pl.CostEstimate(flops=flops, bytes_accessed=moved, transcendentals=0),
    )(*scalars, *arrays)


def swap(value, axis, start, closed):
    count = lax.axis_size(axis)
    pairs = []
    for low in range(start, count if closed else count - 1, 2):
        high = (low + 1) % count
        pairs += [(low, high), (high, low)]
    return lax.ppermute(value, axis, pairs)


def block(query_field, key_field, value_field, out_cotangent):
    band = lax.axis_index("lat")
    edge = (band == 0) | (band == lax.axis_size("lat") - 1)
    bias = jnp.where(edge, FAR, 0.0).astype(F32)[None]
    odd = (lax.axis_index("lon") % 2).astype(jnp.int32)[None]
    field, width = query_field.shape, query_field.shape[-1]
    pairs = width // PAIR

    def named_swap(first, second, axis):
        second = swap(second, axis, 1, axis == "lon")
        first = swap(first, axis, 0, axis == "lon")
        return first, second

    def pack(*bands):
        column = ((len(bands) * CELLS, width), BF16)
        return call(pack_kernel, [odd], list(bands), [column, column], 1 << 20, 2 << 20)

    keys, values = key_field.reshape(BAND, width), value_field.reshape(BAND, width)
    keys_even, keys_odd = named_swap(keys, keys, "lat")
    values_even, values_odd = named_swap(values, values, "lat")
    (queries,) = call(order_kernel, [odd], [query_field, out_cotangent], [((2, BAND, width), BF16)], 1 << 20, 1 << 20)
    queries_even, queries_odd = named_swap(queries, queries, "lat")
    first_k, second_k = named_swap(*pack(keys, keys_even, keys_odd), "lon")
    first_v, second_v = named_swap(*pack(values, values_even, values_odd), "lon")
    around = [queries, keys, keys_even, keys_odd, first_k, second_k]
    around += [values, values_even, values_odd, first_v, second_v]
    att, stats, low = call(
        attend_kernel, [bias, odd], around,
        [(field, BF16), ((pairs, 8, PAIR), F32), ((pairs, CORE + SIDE, 2 * PAIR), BF16)], 1 << 30, 8 << 20,
    )
    stats_even, stats_odd = named_swap(stats, stats, "lat")
    dq, part = call(
        slope_kernel, [odd], [*around, stats, low],
        [(field, BF16), ((2, 2 * BAND, width), F32)], 1 << 30, 8 << 20,
    )
    tile = ((2, CELLS, width), BF16)
    mid, to_first, to_second = call(
        key_kernel, [bias],
        [keys, first_k, second_k, values, first_v, second_v, queries_even, queries_odd, stats_even, stats_odd, part],
        [((2, BAND, width), F32), tile, tile], 1 << 30, 8 << 20,
    )
    from_first, from_second = named_swap(to_first, to_second, "lon")
    dk, dv = call(
        finish_kernel, [odd], [mid, from_first, from_second], [(field, BF16), (field, BF16)], 1 << 20, 2 << 20
    )
    return att, dq, dk, dv


def solution(mesh):
    spec = P("lat", "lon", None)
    return jax.shard_map(block, mesh=mesh, in_specs=(spec,) * 4, out_specs=(spec,) * 4, check_vma=False)
```

```python
import jax
import jax.numpy as jnp
from jax import lax
from jax.experimental import pallas as pl
from jax.experimental.pallas import tpu as pltpu
from jax.sharding import PartitionSpec as P


HEAD_DIM = 64
TILE = 8
CELLS = TILE * TILE
BAND = 2 * CELLS
PAIR = 2 * HEAD_DIM
SCALE = HEAD_DIM**-0.5
FAR = -1e30
F32, BF16 = jnp.float32, jnp.bfloat16
UNROLL = 6


def dot(a, b):
    return jnp.dot(a, b, preferred_element_type=F32)


def tile_order(x, odd):
    west = x[:, :TILE].reshape(CELLS, x.shape[-1])
    east = x[:, TILE:].reshape(CELLS, x.shape[-1])
    return jnp.concatenate([jnp.where(odd, west, east), jnp.where(odd, east, west)], axis=0)


def grid_order(x, odd):
    first = x[:CELLS].reshape(TILE, TILE, x.shape[-1])
    second = x[CELLS:].reshape(TILE, TILE, x.shape[-1])
    return jnp.concatenate([jnp.where(odd, first, second), jnp.where(odd, second, first)], axis=1)


def below(shape, axis, bound):
    return lax.broadcasted_iota(jnp.int32, shape, axis) < bound


def wide(x):
    row = below(x.shape, 0, HEAD_DIM)
    return jnp.concatenate([jnp.where(row, x, 0.0), jnp.where(row, 0.0, x)], axis=1).astype(BF16)


def diagonal(x):
    return jnp.concatenate([x[:HEAD_DIM, :PAIR], x[HEAD_DIM:, PAIR : 2 * PAIR]], axis=0)


def by_head(x):
    return jnp.concatenate(
        [
            jnp.sum(x[:HEAD_DIM], axis=0, keepdims=True),
            jnp.sum(x[HEAD_DIM:], axis=0, keepdims=True),
        ],
        axis=1,
    )


def each_pair(width, step):
    def body(p, carry):
        step(p, pl.ds(pl.multiple_of(p * PAIR, PAIR), PAIR))
        return carry

    lax.fori_loop(0, width // PAIR, body, 0, unroll=UNROLL)


CORE, SIDE = 3 * BAND, 3 * CELLS


def beside_first(rows):
    return (lax.broadcasted_iota(jnp.int32, (rows, 2 * PAIR), 1) & CELLS) == 0


def near(x):
    sides = jnp.where(beside_first(SIDE), x[CORE : CORE + SIDE], x[CORE + SIDE :])
    return jnp.concatenate([x[:CORE], sides], axis=0)


def split(x):
    first, none = beside_first(x.shape[0]), jnp.zeros((), x.dtype)
    return [jnp.where(first, x, none), jnp.where(first, none, x)]


def attend_kernel(
    bias_ref, odd_ref, mine_ref, own_ref, even_ref, odds_ref, first_ref, second_ref, att_ref, stats_ref, low_ref
):
    odd = odd_ref[0] == 1
    refs = (own_ref, even_ref, odds_ref, first_ref, second_ref)

    def step(p, lanes):
        k_all = jnp.concatenate([ref[0, :, lanes] for ref in refs], axis=0)
        v_all = jnp.concatenate([ref[1, :, lanes] for ref in refs], axis=0)
        q_turn = mine_ref[0, :, lanes].astype(F32).T
        g_turn = mine_ref[1, :, lanes].astype(F32).T
        scores = near(dot(k_all, wide(q_turn)))
        cut, last = 2 * BAND, CORE + 2 * CELLS
        bias = bias_ref[0]
        scores = jnp.concatenate(
            [scores[:cut], scores[cut:CORE] + bias, scores[CORE:last], scores[last:] + bias], axis=0
        )
        peak = jnp.max(scores, axis=0, keepdims=True)
        raised = jnp.exp(scores - peak)
        total = jnp.sum(raised, axis=0, keepdims=True)
        low = (raised * (1.0 / total)).astype(BF16)
        low_ref[p] = low
        full = jnp.concatenate([low[:CORE], *split(low[CORE:])], axis=0)
        att_turn = diagonal(dot(v_all.T, full)).astype(BF16).astype(F32)
        att_ref[:, :, lanes] = grid_order(att_turn.T, odd).astype(BF16)
        drift = by_head(g_turn * att_turn)
        log_total = peak + jnp.log(total)
        stats_ref[p] = jnp.concatenate(
            [log_total[:, :PAIR], log_total[:, PAIR:], drift[:, :PAIR], drift[:, PAIR:], jnp.zeros((4, PAIR), F32)],
            axis=0,
        )

    each_pair(mine_ref.shape[-1], step)


def slope_kernel(
    odd_ref, mine_ref, own_ref, even_ref, odds_ref, first_ref, second_ref, stats_ref, low_ref, dq_ref, part_ref
):
    odd = odd_ref[0] == 1
    refs = (own_ref, even_ref, odds_ref, first_ref, second_ref)

    def step(p, lanes):
        k_all = jnp.concatenate([ref[0, :, lanes] for ref in refs], axis=0)
        v_all = jnp.concatenate([ref[1, :, lanes] for ref in refs], axis=0)
        q_mine, g_mine = mine_ref[0, :, lanes], mine_ref[1, :, lanes]
        stats = stats_ref[p]
        drift = jnp.concatenate([stats[2:3], stats[3:4]], axis=1)
        low = low_ref[p]
        slopes = (low.astype(F32) * (near(dot(v_all, wide(g_mine.astype(F32).T))) - drift)).astype(BF16)
        full = jnp.concatenate([slopes[:CORE], *split(slopes[CORE:])], axis=0)
        dq_turn = diagonal(dot(k_all.T, full)) * SCALE
        dq_ref[:, :, lanes] = grid_order(dq_turn.T, odd).astype(BF16)
        lane = below((PAIR, PAIR), 1, HEAD_DIM)
        for which, rows, mine in ((0, slopes, q_mine), (1, low, g_mine)):
            none = jnp.zeros((), BF16)
            tall = jnp.concatenate([jnp.where(lane, mine, none), jnp.where(lane, none, mine)], axis=0)
            rows = jnp.concatenate([rows[:BAND], *split(rows[CORE : CORE + CELLS])], axis=0)
            part_ref[which, :, lanes] = dot(rows, tall)

    each_pair(mine_ref.shape[-1], step)


def key_kernel(
    bias_ref, own_ref, first_ref, second_ref, even_ref, odds_ref, even_stats, odds_stats, part_ref,
    mid_ref, to_first_ref, to_second_ref,
):
    refs = (even_ref, odds_ref)

    def step(p, lanes):
        low_lane = below((PAIR, PAIR), 1, CELLS)
        low_row = below((PAIR, PAIR), 0, HEAD_DIM)

        def keys(which):
            own = own_ref[which, :, lanes].astype(F32).T
            both = jnp.concatenate(
                [first_ref[which, :CELLS, lanes], second_ref[which, :CELLS, lanes]], axis=0
            ).astype(F32).T
            turned = pltpu.roll(both, CELLS, axis=1)
            block = low_row == low_lane
            first = jnp.where(block, jnp.where(low_lane, both, turned), 0.0).astype(BF16)
            second = jnp.where(block, jnp.where(low_lane, turned, both), 0.0).astype(BF16)
            return jnp.concatenate([wide(own), first, second], axis=1)

        def beside(x):
            sides = [
                x[at * CELLS : (at + 1) * CELLS, (2 + at % 2) * PAIR : (3 + at % 2) * PAIR] for at in range(4)
            ]
            return jnp.concatenate([x[:, : 2 * PAIR], jnp.concatenate(sides, axis=0)], axis=1)

        def spread(x):
            x = x.astype(BF16)
            none = jnp.zeros((CELLS, PAIR), BF16)
            sides = [x[at * CELLS : (at + 1) * CELLS, 2 * PAIR :] for at in range(4)]
            first = jnp.concatenate([none if at % 2 else sides[at] for at in range(4)], axis=0)
            second = jnp.concatenate([sides[at] if at % 2 else none for at in range(4)], axis=0)
            return jnp.concatenate([x[:, : 2 * PAIR], first, second], axis=1)

        stats = [ref[p] for ref in (even_stats, odds_stats)]
        columns = jnp.concatenate(stats + [jnp.zeros((PAIR - 16, PAIR), F32)], axis=0).T

        def column(base):
            rows = []
            for at in range(2):
                head0 = jnp.broadcast_to(columns[:, 8 * at + base : 8 * at + base + 1], (PAIR, PAIR))
                head1 = jnp.broadcast_to(columns[:, 8 * at + base + 1 : 8 * at + base + 2], (PAIR, PAIR))
                rows.append(jnp.concatenate([head0, head1, jnp.where(low_lane, head0, head1)], axis=1))
            return jnp.concatenate(rows, axis=0)

        def store(which, x):
            part = part_ref[which, :, lanes]
            mid_ref[which, :, lanes] = part[:BAND] + diagonal(x).T
            first, second = x[:, 2 * PAIR : 3 * PAIR], x[:, 3 * PAIR :]
            first = jnp.where(low_row, first, pltpu.roll(first, CELLS, axis=1))
            second = jnp.where(low_row, pltpu.roll(second, CELLS, axis=1), second)
            both = (part[BAND:] + jnp.where(low_lane, first, second).T).astype(BF16)
            to_first_ref[which, :, lanes] = both[:CELLS]
            to_second_ref[which, :, lanes] = both[CELLS:]

        q_all = jnp.concatenate([ref[0, :, lanes] for ref in refs], axis=0)
        g_all = jnp.concatenate([ref[1, :, lanes] for ref in refs], axis=0)
        scores = beside(dot(q_all, keys(0)))
        scores = jnp.concatenate([scores[:BAND], scores[BAND:] + bias_ref[0]], axis=0)
        weights = jnp.exp(scores - column(0))
        store(1, dot(g_all.T, spread(weights)))
        slopes = weights * (beside(dot(g_all, keys(1))) - column(2))
        store(0, dot(q_all.T, spread(slopes)))

    each_pair(own_ref.shape[-1], step)


def order_kernel(odd_ref, q_ref, g_ref, out_ref):
    odd = odd_ref[0] == 1
    out_ref[0] = (tile_order(q_ref[...].astype(F32), odd) * SCALE).astype(BF16)
    out_ref[1] = tile_order(g_ref[...].astype(F32), odd).astype(BF16)


def pack_kernel(odd_ref, *refs):
    odd = odd_ref[0] == 1
    bands, (first_ref, second_ref) = refs[:-2], refs[-2:]
    for which in range(2):
        for at, ref in enumerate(bands):
            x = ref[which].astype(F32).reshape(TILE, 2 * TILE, ref.shape[-1])
            ordered = tile_order(x, odd).astype(BF16)
            first_ref[which, at * CELLS : (at + 1) * CELLS] = ordered[:CELLS]
            second_ref[which, at * CELLS : (at + 1) * CELLS] = ordered[CELLS:]


def append_kernel(odd_ref, near_first_ref, near_second_ref, odds_ref, first_ref, second_ref):
    odd = odd_ref[0] == 1
    near = 2 * CELLS
    for which in range(2):
        first_ref[which, :near] = near_first_ref[which]
        second_ref[which, :near] = near_second_ref[which]
        x = odds_ref[which].astype(F32).reshape(TILE, 2 * TILE, odds_ref.shape[-1])
        ordered = tile_order(x, odd).astype(BF16)
        first_ref[which, near:] = ordered[:CELLS]
        second_ref[which, near:] = ordered[CELLS:]


def finish_kernel(odd_ref, mid_ref, first_ref, second_ref, dk_ref, dv_ref):
    odd = odd_ref[0] == 1
    for which, out in ((0, dk_ref), (1, dv_ref)):
        sides = jnp.concatenate([first_ref[which], second_ref[which]], axis=0).astype(F32)
        mid = mid_ref[which].reshape(TILE, 2 * TILE, mid_ref.shape[-1])
        out[...] = (mid + grid_order(sides, odd)).astype(BF16)


def call(kernel, scalars, arrays, outs, flops, moved):
    return pl.pallas_call(
        kernel,
        in_specs=[pl.BlockSpec(memory_space=pltpu.SMEM)] * len(scalars)
        + [pl.BlockSpec(memory_space=pltpu.VMEM)] * len(arrays),
        out_specs=[pl.BlockSpec(memory_space=pltpu.VMEM)] * len(outs),
        out_shape=[jax.ShapeDtypeStruct(*out) for out in outs],
        compiler_params=pltpu.CompilerParams(vmem_limit_bytes=20 << 20),
        cost_estimate=pl.CostEstimate(flops=flops, bytes_accessed=moved, transcendentals=0),
    )(*scalars, *arrays)


def swap(value, axis, start, closed):
    count = lax.axis_size(axis)
    pairs = []
    for low in range(start, count if closed else count - 1, 2):
        high = (low + 1) % count
        pairs += [(low, high), (high, low)]
    return lax.ppermute(value, axis, pairs)


def block(query_field, key_field, value_field, out_cotangent):
    band = lax.axis_index("lat")
    edge = (band == 0) | (band == lax.axis_size("lat") - 1)
    bias = jnp.where(edge, FAR, 0.0).astype(F32)[None]
    odd = (lax.axis_index("lon") % 2).astype(jnp.int32)[None]
    field, width = query_field.shape, query_field.shape[-1]
    pairs = width // PAIR

    def named_swap(first, second, axis):
        second = swap(second, axis, 1, axis == "lon")
        first = swap(first, axis, 0, axis == "lon")
        return first, second

    def pack(*bands):
        column = ((2, len(bands) * CELLS, width), BF16)
        return call(pack_kernel, [odd], list(bands), [column, column], 1 << 20, 2 << 20)

    keys = jnp.stack([key_field.reshape(BAND, width), value_field.reshape(BAND, width)])
    keys_even, keys_odd = named_swap(keys, keys, "lat")
    (queries,) = call(order_kernel, [odd], [query_field, out_cotangent], [((2, BAND, width), BF16)], 1 << 20, 1 << 20)
    queries_even, queries_odd = named_swap(queries, queries, "lat")
    near_first, near_second = pack(keys, keys_even)
    column = ((2, 3 * CELLS, width), BF16)
    first, second = call(append_kernel, [odd], [near_first, near_second, keys_odd], [column, column], 1 << 20, 2 << 20)
    first, second = named_swap(first, second, "lon")
    around = [queries, keys, keys_even, keys_odd, first, second]
    att, stats, low = call(
        attend_kernel, [bias, odd], around,
        [(field, BF16), ((pairs, 8, PAIR), F32), ((pairs, CORE + SIDE, 2 * PAIR), BF16)], 1 << 30, 8 << 20,
    )
    stats_even, stats_odd = named_swap(stats, stats, "lat")
    dq, part = call(
        slope_kernel, [odd], [*around, stats, low],
        [(field, BF16), ((2, 2 * BAND, width), F32)], 1 << 30, 8 << 20,
    )
    tile = ((2, CELLS, width), BF16)
    mid, to_first, to_second = call(
        key_kernel, [bias],
        [keys, first, second, queries_even, queries_odd, stats_even, stats_odd, part],
        [((2, BAND, width), F32), tile, tile], 1 << 30, 8 << 20,
    )
    from_first, from_second = named_swap(to_first, to_second, "lon")
    dk, dv = call(
        finish_kernel, [odd], [mid, from_first, from_second], [(field, BF16), (field, BF16)], 1 << 20, 2 << 20
    )
    return att, dq, dk, dv


def solution(mesh):
    spec = P("lat", "lon", None)
    return jax.shard_map(block, mesh=mesh, in_specs=(spec,) * 4, out_specs=(spec,) * 4, check_vma=False)
```
